32 devices in a mesh: segment: 2 (over x), seq: 4 (over y, core), head: 4 (over z).
Axes of the slice: x: 2, y: 2, z: 4, core: 2. Of those that a mesh axis runs over, the one named last changes fastest.
Arguments:
- stream: bfloat16 [2, 512, 4096], P(None, 'seq', 'head'), may hold values from -6 to 6
- in_gain: float32 [2, 4096], P('segment'), may hold values from 0.25 to 1.75
- w_qkv: bfloat16 [2, 4096, 4, 3, 512], P('segment', None, 'head'), may hold values from -0.09375 to 0.09375
- qk_gain: float32 [2, 4, 2, 512], P('segment', 'head'), may hold values from 0.25 to 1.75
- w_one: bfloat16 [2, 4, 512, 768], P('segment', 'head'), may hold values from -0.25 to 0.25
- w_three: bfloat16 [2, 4, 512, 768], P('segment', 'head'), may hold values from -0.25 to 0.25
- w_two: bfloat16 [2, 4, 768, 512], P('segment', 'head'), may hold values from -0.21875 to 0.21875
- token_rate: float32 [2, 2, 512], P('segment', None, 'seq'), may hold values from 0.05 to 1
- out_gain: float32 [2, 4, 512], P('segment', 'head'), may hold values from 0.25 to 1.75
- w_out: bfloat16 [2, 4, 512, 4096], P('segment', 'head'), may hold values from -0.125 to 0.125
Outputs:
- sections_out: bfloat16 [2, 2, 512, 4096], P('segment', None, 'seq', 'head')
The draws below stay inside these ranges and needn't reach their ends.
All inputs are finite; a program needn't handle non-finite values.
Results may differ from the reference program's by a relative error of at most 0.038.
Values may be sent and summed in bfloat16 or wider, within the bound.
A program may use at most 128 MiB of HBM per device.

```python
import math
import jax
import jax.numpy as jnp
from jax import lax

DH = 512
FF = 768
HEADS = 4
DM = 4096
SECTIONS = 2
SPANS = 2
NS_STEPS = 2
TOKENS = 512
N_SEQ = 4


def block_levels(stream_key, dims, split, least, high):
    gain = 1.0
    for axis_at, blocks in split:
        steps = jax.random.uniform(jax.random.fold_in(jax.random.fold_in(stream_key, 6), axis_at), (blocks,), jnp.float32, least / len(split), high / len(split))
        gain = gain * jnp.repeat(jnp.exp(steps), dims[axis_at] // blocks).reshape((-1,) + (1,) * (len(dims) - 1 - axis_at))
    return gain


def gaussian(own_key, shape, spread, limit, pieces=(), held_as=jnp.bfloat16):
    entries = jax.random.normal(own_key, shape, jnp.float32) * spread
    if len(pieces) > 0:
        entries = block_levels(own_key, shape, pieces, -0.22, 0.18) * entries
    return jnp.clip(entries, min=-limit, max=limit).astype(held_as)


def setup_inputs(seed: int = 0) -> dict:
    keys = jax.random.split(jax.random.key(seed), 11)
    stream = gaussian(keys[0], (SPANS, TOKENS, DM), 1.0, 6.0, ((1, 4), (2, 4)))
    in_gain = jnp.clip(1.0 + 0.15 * jax.random.normal(keys[1], (SECTIONS, DM), jnp.float32), 0.25, 1.75)
    w_qkv = gaussian(keys[2], (SECTIONS, DM, HEADS, 3, DH), DM ** -0.5, 0.09375, ((0, 2), (2, 4)))
    qk_gain = jnp.clip(1.0 + 0.15 * jax.random.normal(keys[3], (SECTIONS, HEADS, 2, DH), jnp.float32), 0.25, 1.75)
    w_one = gaussian(keys[4], (SECTIONS, HEADS, DH, FF), DH ** -0.5, 0.25, ((0, 2), (1, 4)))
    w_three = gaussian(keys[5], (SECTIONS, HEADS, DH, FF), DH ** -0.5, 0.25, ((0, 2), (1, 4)))
    w_two = gaussian(keys[6], (SECTIONS, HEADS, FF, DH), FF ** -0.5, 0.21875, ((0, 2), (1, 4)))
    token_rate = jnp.clip(jnp.exp(math.log(1.0) - 2.9957323 * jax.random.uniform(keys[7], (SECTIONS, SPANS, TOKENS), jnp.float32) ** block_levels(keys[7], (SECTIONS, SPANS, TOKENS), ((0, 2), (2, 4)), -0.2, 0.2)), 0.05, 1.0)
    out_gain = jnp.clip(1.0 + 0.15 * jax.random.normal(keys[8], (SECTIONS, HEADS, DH), jnp.float32), 0.25, 1.75)
    w_out = gaussian(keys[9], (SECTIONS, HEADS, DH, DM), (HEADS * DH) ** -0.5, 0.125, ((0, 2), (1, 4)))
    return dict(stream=stream, in_gain=in_gain, w_qkv=w_qkv, qk_gain=qk_gain, w_one=w_one, w_three=w_three, w_two=w_two, token_rate=token_rate, out_gain=out_gain, w_out=w_out)


ns_first = 3.4445
ns_second = -4.775
ns_third = 2.0315
update_step = 1.0
norm_eps = 1e-06
grad_eps = 1e-07

def rms_scale(values):
    return values * lax.rsqrt(lax.optimization_barrier(jnp.mean(values * values, axis=-1, keepdims=True)) + norm_eps)

def orthogonalize(gradient):
    current = (gradient / (jnp.sqrt(jnp.sum(gradient * gradient)) + grad_eps)).astype(jnp.bfloat16)
    row_count = gradient.shape[0]
    column_count = gradient.shape[1]
    for sweep_index in range(NS_STEPS):
        blocks = current.astype(jnp.float32).reshape(row_count, N_SEQ, column_count // N_SEQ)
        partial_grams = jnp.einsum('inb,jnb->nij', blocks, blocks).astype(jnp.bfloat16)
        gram_matrix = lax.optimization_barrier(jnp.sum(partial_grams.astype(jnp.float32), axis=0)).astype(jnp.bfloat16)
        square = jnp.dot(gram_matrix, gram_matrix, preferred_element_type=jnp.float32)
        mixing = (ns_second * gram_matrix.astype(jnp.float32) + ns_third * square).astype(jnp.bfloat16)
        current = (ns_first * current.astype(jnp.float32) + jnp.dot(mixing, current, preferred_element_type=jnp.float32)).astype(jnp.bfloat16)
    return current

def renormalize(weights, target_norms):
    return weights * (target_norms / (jnp.sqrt(lax.optimization_barrier(jnp.sum(weights * weights, axis=0))) + norm_eps))

def head_update(queries, key_rows, out_grad, fast, initial_norms):
    gate_fast, up_fast, down_fast = fast
    gate_low = gate_fast.astype(jnp.bfloat16)
    up_low = up_fast.astype(jnp.bfloat16)
    down_low = down_fast.astype(jnp.bfloat16)
    pre_gate = jnp.dot(key_rows, gate_low, preferred_element_type=jnp.float32)
    pre_up = jnp.dot(key_rows, up_low, preferred_element_type=jnp.float32)
    sigmoid_gate = jax.nn.sigmoid(pre_gate)
    gated = pre_gate * sigmoid_gate
    hidden = (gated * pre_up).astype(jnp.bfloat16)
    backward = jnp.dot(out_grad, down_low.T, preferred_element_type=jnp.float32)
    grad_gate = (backward * pre_up * sigmoid_gate * (1.0 + pre_gate * (1.0 - sigmoid_gate))).astype(jnp.bfloat16)
    grad_up = (backward * gated).astype(jnp.bfloat16)
    grad_first = jnp.dot(key_rows.T, grad_gate, preferred_element_type=jnp.float32)
    grad_third = jnp.dot(key_rows.T, grad_up, preferred_element_type=jnp.float32)
    grad_second = jnp.dot(out_grad.T, hidden, preferred_element_type=jnp.float32)
    gate_fast = renormalize(gate_fast - update_step * orthogonalize(grad_first).astype(jnp.float32), initial_norms[0])
    up_fast = renormalize(up_fast - update_step * orthogonalize(grad_third).astype(jnp.float32), initial_norms[1])
    down_fast = renormalize(down_fast - update_step * orthogonalize(grad_second).astype(jnp.float32).T, initial_norms[2])
    gate_out = jnp.dot(queries, gate_fast, precision=lax.Precision.HIGHEST)
    up_out = jnp.dot(queries, up_fast, precision=lax.Precision.HIGHEST)
    output = jnp.dot(jax.nn.silu(gate_out) * up_out, down_fast, precision=lax.Precision.HIGHEST)
    return (output, (gate_fast, up_fast, down_fast))

def run_section(residual, gain_row, qkv_weights, qk_gains, rate_row, out_gains, out_weights, fasts, norms):
    values = residual.astype(jnp.float32)
    normed = (rms_scale(values) * gain_row).astype(jnp.bfloat16)
    projected = jnp.dot(normed, qkv_weights.reshape(DM, HEADS * 3 * DH), preferred_element_type=jnp.float32)
    projected = projected.reshape(TOKENS, HEADS, 3, DH)
    mixed = jnp.zeros((TOKENS, DM), jnp.float32)
    new_fasts = []
    for head_index in range(HEADS):
        queries = rms_scale(projected[:, head_index, 0]) * qk_gains[head_index, 0]
        key_rows = (rms_scale(projected[:, head_index, 1]) * qk_gains[head_index, 1]).astype(jnp.bfloat16)
        out_grad = (-rate_row[:, None] * projected[:, head_index, 2]).astype(jnp.bfloat16)
        output, updated = head_update(queries, key_rows, out_grad, fasts[head_index], norms[head_index])
        normed_out = (rms_scale(output) * out_gains[head_index]).astype(jnp.bfloat16)
        mixed = mixed + jnp.dot(normed_out, out_weights[head_index], preferred_element_type=jnp.float32)
        new_fasts.append(updated)
    return ((values + mixed).astype(jnp.bfloat16), new_fasts)

def reference(stream, in_gain, w_qkv, qk_gain, w_one, w_three, w_two, token_rate, out_gain, w_out):
    results = []
    for section in range(SECTIONS):
        fasts = []
        norms = []
        for head_index in range(HEADS):
            weights = (w_one[section, head_index].astype(jnp.float32), w_three[section, head_index].astype(jnp.float32), w_two[section, head_index].astype(jnp.float32))
            fasts.append(weights)
            norms.append(tuple((jnp.sqrt(lax.optimization_barrier(jnp.sum(matrix * matrix, axis=0))) for matrix in weights)))
        section_out = []
        for span_index in range(SPANS):
            if section == 0:
                source = stream[span_index]
            else:
                source = results[section - 1][span_index]
            result, fasts = run_section(source, in_gain[section], w_qkv[section], qk_gain[section], token_rate[section, span_index], out_gain[section], w_out[section], fasts, norms)
            section_out.append(result)
        results.append(section_out)
    return jnp.stack([jnp.stack(section_out) for section_out in results])
```

```python
import functools

import jax
import jax.numpy as jnp
from jax import lax
from jax.experimental import pallas as pl
from jax.experimental.pallas import tpu as pltpu
from jax.sharding import PartitionSpec as P

NS_STEPS = 2

ns_first = 3.4445
ns_second = -4.775
ns_third = 2.0315
update_step = 1.0
norm_eps = 1e-06
grad_eps = 1e-07


def rms_scale(values):
    return values * lax.rsqrt(jnp.mean(values * values, axis=-1, keepdims=True) + norm_eps)


def dot(left, right):
    return jnp.dot(left, right, preferred_element_type=jnp.float32)


def contract(left, right, dims):
    return lax.dot_general(
        left, right, ((dims[:1], dims[1:]), ((), ())), preferred_element_type=jnp.float32
    )


def signal(semaphore, target):
    pl.semaphore_signal(
        semaphore, inc=1, device_id=target, device_id_type=pl.DeviceIdType.MESH
    )


def remote(source, target, send_sem, recv_sem, device):
    return pltpu.make_async_remote_copy(
        src_ref=source,
        dst_ref=target,
        send_sem=send_sem,
        recv_sem=recv_sem,
        device_id=device,
        device_id_type=pl.DeviceIdType.MESH,
    )


def step_kernel(
    segments,
    devices,
    heads,
    chunks,
    stream_hbm,
    in_gain_ref,
    qkv_hbm,
    qk_gain_ref,
    gate_hbm,
    up_hbm,
    down_hbm,
    rate_ref,
    out_gain_ref,
    out_hbm,
    result_ref,
    qkv,
    out_weights,
    wide_init,
    down_init,
    whole,
    scaled,
    sums,
    both,
    queries,
    rights,
    work,
    state,
    wide_norms,
    down_norm,
    terms,
    slots,
    qkv_sems,
    load_sems,
    own_sems,
    spread_sends,
    arrivals,
    far_sends,
    far_recvs,
    near_sends,
    near_recvs,
    term_sends,
    term_recvs,
    hop_sends,
    relay_sends,
):
    segment = lax.axis_index("segment")
    place_seq = lax.axis_index("seq")
    me = lax.axis_index("head")
    spans, rows, width = result_ref.shape
    features = whole.shape[2]
    chips = devices // 2
    chip, core = place_seq // 2, lax.rem(place_seq, 2)
    partner = {"seq": 2 * chip + 1 - core}
    piece = rows // chunks
    last_segment = segments - 1

    loads = [pltpu.make_async_copy(qkv_hbm.at[part], qkv.at[part], qkv_sems.at[part]) for part in range(3)]
    for part in (1, 2, 0):
        loads[part].start()
    fast_loads = [
        pltpu.make_async_copy(gate_hbm, wide_init.at[0], load_sems.at[0]),
        pltpu.make_async_copy(up_hbm, wide_init.at[1], load_sems.at[1]),
        pltpu.make_async_copy(down_hbm, down_init, load_sems.at[2]),
    ]
    out_load = pltpu.make_async_copy(out_hbm, out_weights, load_sems.at[3])
    for copy in fast_loads + [out_load]:
        copy.start()

    def other_head(step):
        return lax.rem(me + step, heads)

    barrier = pltpu.get_barrier_semaphore()
    for away in range(segments):
        for step in range(heads):
            if away or step:
                signal(barrier, {"segment": lax.rem(segment + away, segments), "head": other_head(step)})
    for step in range(1, chips):
        signal(barrier, {"seq": 2 * lax.rem(chip + step, chips) + core})
    signal(barrier, partner)
    pl.semaphore_wait(barrier, segments * heads - 1 + chips)

    def columns_of(origin):
        return pl.ds(pl.multiple_of(origin * width, width), width)

    def rows_of(chunk):
        if isinstance(chunk, int):
            return pl.ds(chunk * piece, piece)
        return pl.ds(pl.multiple_of(chunk * piece, piece), piece)

    def place(span, origin, chunk):
        return whole.at[span, rows_of(chunk), columns_of(origin)]

    def spread(span, step, chunk):
        return remote(
            stream_hbm.at[span, rows_of(chunk), :],
            place(span, me, chunk),
            spread_sends.at[span, step, chunk],
            arrivals.at[span, me, chunk],
            {"segment": 0, "head": other_head(step)},
        )

    def each_spread(action):
        for span in range(spans):
            for chunk in range(chunks):

                @pl.when(segment == chunk * segments // chunks)
                def _():
                    for step in range(1, heads):
                        action(spread(span, step, chunk))

    each_spread(lambda copy: copy.start())

    def own_copy(span):
        return pltpu.make_async_copy(
            stream_hbm.at[span], whole.at[span, :, columns_of(me)], own_sems.at[span]
        )

    @pl.when(segment == 0)
    def _():
        for span in range(spans):
            own_copy(span).start()

    for copy in fast_loads:
        copy.wait()
    for index in range(2):
        work[index] = wide_init[index]
        wide = wide_init[index].astype(jnp.float32)
        state[index] = wide
        wide_norms[index] = jnp.sqrt(jnp.sum(wide * wide, axis=0, keepdims=True))
    down = down_init[...].T
    work[2] = down
    down = down.astype(jnp.float32)
    state[2] = down
    down_norm[...] = jnp.sqrt(jnp.sum(down * down, axis=1, keepdims=True))

    def arrival(span, origin, chunk):
        return remote(
            place(span, origin, chunk),
            place(span, origin, chunk),
            hop_sends.at[span, chunk],
            arrivals.at[span, origin, chunk],
            {"head": other_head(1)},
        )

    def relay_copy(span, step, chunk):
        return remote(
            place(span, me, chunk),
            place(span, me, chunk),
            relay_sends.at[span, step, chunk],
            arrivals.at[span, me, chunk],
            {"head": other_head(step)},
        )

    def relay(span, chunk):
        arrival(span, me, chunk).wait_recv()
        for step in range(1, heads):
            relay_copy(span, step, chunk).start()

    def project_keys(span):
        sums[0] = jnp.zeros(sums.shape[1:], jnp.float32)
        sums[1] = jnp.zeros(sums.shape[1:], jnp.float32)

        def block(step, squares):
            origin = other_head(step)

            @pl.when(step > 0)
            def _():
                for chunk in range(chunks):
                    arrival(span, origin, chunk).wait_recv()

            here = columns_of(origin)
            values = whole[span, :, here].astype(jnp.float32)
            scaled[:, here] = (values * in_gain_ref[:, here]).astype(jnp.bfloat16)
            sums[0] += dot(scaled[:, here], qkv[1, here, :])
            sums[1] += dot(scaled[:, here], qkv[2, here, :])
            return squares + jnp.sum(values * values, axis=1, keepdims=True)

        squares = lax.fori_loop(0, heads, block, jnp.zeros((rows, 1), jnp.float32))
        return lax.rsqrt(squares * (1.0 / features) + norm_eps)

    def rows_at(origin, count=1):
        return pl.ds(pl.multiple_of(origin * rows, rows), count * rows)

    def far_copy(span, part, step):
        return remote(
            both.at[span, part, rows_at(place_seq), :],
            both.at[span, part, rows_at(place_seq), :],
            far_sends.at[span, part, step],
            far_recvs.at[span, part, step],
            {"seq": 2 * lax.rem(chip + step, chips) + core},
        )

    def near_copy(span, part, step):
        origin = 2 * lax.rem(chip + chips - step, chips) + core
        return remote(
            both.at[span, part, rows_at(origin), :],
            both.at[span, part, rows_at(origin), :],
            near_sends.at[span, part, step],
            near_recvs.at[span, part, step],
            partner,
        )

    def project(span):
        scale = project_keys(span)
        own = rows_at(place_seq)
        both[span, 0, own, :] = (rms_scale(sums[0] * scale) * qk_gain_ref[1:2, :]).astype(jnp.bfloat16)
        diagonal = lax.broadcasted_iota(jnp.int32, (rows, rows), 0) == lax.broadcasted_iota(
            jnp.int32, (rows, rows), 1
        )
        rates = jnp.sum(
            jnp.where(diagonal, rate_ref[pl.ds(span, 1), :], 0.0), axis=1, keepdims=True
        )
        both[span, 1, own, :] = (-rates * (sums[1] * scale)).astype(jnp.bfloat16)
        for part in range(2):
            for step in range(1, chips):
                far_copy(span, part, step).start()
        for part in range(2):
            near_copy(span, part, 0).start()
        sums[0] = dot(scaled[...], qkv[0])
        queries[...] = (rms_scale(sums[0] * scale) * qk_gain_ref[0:1, :]).astype(jnp.bfloat16)

    def finish(span, chunk):
        here = rows_of(chunk)
        total = whole[span, here, columns_of(me)].astype(jnp.float32) + terms[
            span, me, here, :
        ].astype(jnp.float32)
        for step in range(1, heads):
            origin = other_head(step)
            term_arrival(span, origin, chunk).wait_recv()
            total += slots[span, origin, here, :].astype(jnp.float32)
        result_ref[span, here, :] = total.astype(jnp.bfloat16)

        @pl.when(segment < last_segment)
        def _():
            hop(span, chunk).start()

    def term_copy(span, step, chunk):
        target = other_head(step)
        return remote(
            terms.at[span, target, rows_of(chunk), :],
            slots.at[span, me, rows_of(chunk), :],
            term_sends.at[span, step, chunk],
            term_recvs.at[span, me, chunk],
            {"head": target},
        )

    def term_arrival(span, origin, chunk):
        return remote(
            slots.at[span, origin, rows_of(chunk), :],
            slots.at[span, origin, rows_of(chunk), :],
            hop_sends.at[span, chunk],
            term_recvs.at[span, origin, chunk],
            {"head": other_head(1)},
        )

    def hop(span, chunk):
        return remote(
            result_ref.at[span, rows_of(chunk), :],
            place(span, me, chunk),
            hop_sends.at[span, chunk],
            arrivals.at[span, me, chunk],
            {"segment": segment + 1},
        )

    def between(span, chunk):
        @pl.when(span > 0)
        def _():
            finish(span - 1, chunk)

        @pl.when((segment > 0) & (span + 1 < spans))
        def _():
            relay(span + 1, chunk)

    def gradients(span, step):
        for part in range(2):

            @pl.when(step > 0)
            def _():
                remote(
                    both.at[span, part, rows_at(2 * lax.rem(chip + chips - step, chips) + core), :],
                    both.at[span, part, rows_at(2 * lax.rem(chip + chips - step, chips) + core), :],
                    far_sends.at[span, part, step],
                    far_recvs.at[span, part, step],
                    partner,
                ).wait_recv()
                near_copy(span, part, step).start()

        origin = lax.rem(chip + chips - step, chips)
        for part in range(2):
            twin = rows_at(2 * origin + 1 - core)
            remote(
                both.at[span, part, twin, :],
                both.at[span, part, twin, :],
                near_sends.at[span, part, step],
                near_recvs.at[span, part, step],
                partner,
            ).wait_recv()
        here = rows_at(2 * origin, 2)
        keys = both[span, 0, here, :]
        grads = both[span, 1, here, :]
        pre_gate = dot(keys, work[0])
        pre_up = dot(keys, work[1])
        backward = dot(grads, work[2])
        sigmoid_gate = jax.nn.sigmoid(pre_gate)
        gated = pre_gate * sigmoid_gate
        rights[0, here, :] = (
            backward * pre_up * sigmoid_gate * (1.0 + pre_gate * (1.0 - sigmoid_gate))
        ).astype(jnp.bfloat16)
        rights[1, here, :] = (backward * gated).astype(jnp.bfloat16)
        rights[2, here, :] = (gated * pre_up).astype(jnp.bfloat16)

    def orthogonalize(span, index):
        gradient = contract(both[span, index // 2], rights[index], (0, 0))
        scale = 1.0 / (jnp.sqrt(jnp.sum(gradient * gradient, keepdims=True)) + grad_eps)
        work[index] = (gradient * scale).astype(jnp.bfloat16)

        def sweep(step, inner):
            current = work[index]
            gram_matrix = contract(current, current, (1, 1)).astype(jnp.bfloat16)
            square = dot(gram_matrix, gram_matrix)
            mixing = (ns_second * gram_matrix.astype(jnp.float32) + ns_third * square).astype(
                jnp.bfloat16
            )
            work[index] = (ns_first * current.astype(jnp.float32) + dot(mixing, current)).astype(
                jnp.bfloat16
            )
            return inner

        lax.fori_loop(0, NS_STEPS, sweep, 0)

    def update():
        for index, axis, target in (
            (0, 0, wide_norms[0]),
            (1, 0, wide_norms[1]),
            (2, 1, down_norm[...]),
        ):
            moved = state[index] - update_step * work[index].astype(jnp.float32)
            length = jnp.sqrt(jnp.sum(moved * moved, axis=axis, keepdims=True)) + norm_eps
            fresh = moved * (target / length)
            work[index] = fresh.astype(jnp.bfloat16)
            state[index] = fresh

    def read_out(span):
        gate_out = dot(queries[...], work[0])
        up_out = dot(queries[...], work[1])
        inner = (gate_out * jax.nn.sigmoid(gate_out) * up_out).astype(jnp.bfloat16)
        output = contract(inner, work[2], (1, 1))
        normed_out = (rms_scale(output) * out_gain_ref[...]).astype(jnp.bfloat16)

        def term(origin, carry):
            terms[span, origin] = dot(normed_out, out_weights[:, columns_of(origin)]).astype(
                jnp.bfloat16
            )
            return carry

        lax.fori_loop(0, heads, term, 0)
        for chunk in range(chunks):
            for step in range(1, heads):
                term_copy(span, step, chunk).start()

    @pl.when(segment == 0)
    def _():
        for span in range(spans):
            own_copy(span).wait()

    @pl.when(segment > 0)
    def _():
        for chunk in range(chunks):
            relay(0, chunk)

    for part in (1, 2, 0):
        loads[part].wait()
    out_load.wait()

    def block(span, carry):
        project(span)

        def gradient_step(step, inner):
            gradients(span, step)
            return inner

        lax.fori_loop(0, chips, gradient_step, 0)
        between(span, 0)

        def orthogonal_step(index, inner):
            orthogonalize(span, index)

            @pl.when(index + 1 < chunks)
            def _():
                between(span, index + 1)

            return inner

        lax.fori_loop(0, 3, orthogonal_step, 0)
        update()
        read_out(span)
        return carry

    lax.fori_loop(0, spans, block, 0)
    for chunk in range(chunks):
        finish(spans - 1, chunk)

    each_spread(lambda copy: copy.wait_send())

    def drain(span, carry):
        for chunk in range(chunks):
            for step in range(1, heads):
                term_copy(span, step, chunk).wait_send()

            @pl.when(segment > 0)
            def _():
                for step in range(1, heads):
                    relay_copy(span, step, chunk).wait_send()

            @pl.when(segment < last_segment)
            def _():
                hop(span, chunk).wait_send()

        for part in range(2):
            for step in range(1, chips):
                far_copy(span, part, step).wait_send()
            for step in range(chips):
                near_copy(span, part, step).wait_send()
        return carry

    lax.fori_loop(0, spans, drain, 0)


def shards(stream, in_gain, w_qkv, qk_gain, w_one, w_three, w_two, token_rate, out_gain, w_out):
    segments = lax.axis_size("segment")
    devices = lax.axis_size("seq")
    heads = lax.axis_size("head")
    spans, rows, width = stream.shape
    features = w_qkv.shape[1]
    inner, wide = w_one.shape[2:]
    tokens = devices * rows
    chunks = 4
    vmem = pl.BlockSpec(memory_space=pltpu.VMEM)
    anywhere = pl.BlockSpec(memory_space=pl.ANY)
    low = jnp.bfloat16
    dma = pltpu.SemaphoreType.DMA
    result = pl.pallas_call(
        functools.partial(step_kernel, segments, devices, heads, chunks),
        name="step",
        out_shape=jax.ShapeDtypeStruct(stream.shape, low),
        in_specs=[anywhere, vmem, anywhere, vmem, anywhere, anywhere, anywhere, vmem, vmem, anywhere],
        out_specs=vmem,
        scratch_shapes=[
            pltpu.VMEM((3, features, inner), low),
            pltpu.VMEM((inner, features), low),
            pltpu.VMEM((2, inner, wide), low),
            pltpu.VMEM((wide, inner), low),
            pltpu.VMEM((spans, rows, features), low),
            pltpu.VMEM((rows, features), low),
            pltpu.VMEM((2, rows, inner), jnp.float32),
            pltpu.VMEM((spans, 2, tokens, inner), low),
            pltpu.VMEM((rows, inner), low),
            pltpu.VMEM((3, tokens, wide), low),
            pltpu.VMEM((3, inner, wide), low),
            pltpu.VMEM((3, inner, wide), jnp.float32),
            pltpu.VMEM((2, 1, wide), jnp.float32),
            pltpu.VMEM((inner, 1), jnp.float32),
            pltpu.VMEM((spans, heads, rows, width), low),
            pltpu.VMEM((spans, heads, rows, width), low),
            dma((3,)),
            dma((4,)),
            dma((spans,)),
            dma((spans, heads, chunks)),
            dma((spans, heads, chunks)),
            dma((spans, 2, devices // 2)),
            dma((spans, 2, devices // 2)),
            dma((spans, 2, devices // 2)),
            dma((spans, 2, devices // 2)),
            dma((spans, heads, chunks)),
            dma((spans, heads, chunks)),
            dma((spans, chunks)),
            dma((spans, heads, chunks)),
        ],
        compiler_params=pltpu.CompilerParams(
            collective_id=0, has_side_effects=True, vmem_limit_bytes=67043328
        ),
    )(
        stream,
        in_gain,
        jnp.transpose(w_qkv[0, :, 0], (1, 0, 2)),
        qk_gain[0, 0],
        w_one[0, 0],
        w_three[0, 0],
        w_two[0, 0],
        token_rate[0],
        out_gain[0, :1],
        w_out[0, 0],
    )
    return result[None]


def solution(mesh):
    placed = (
        P(None, "seq", "head"),
        P("segment", None),
        P("segment", None, "head", None, None),
        P("segment", "head", None, None),
        P("segment", "head", None, None),
        P("segment", "head", None, None),
        P("segment", "head", None, None),
        P("segment", None, "seq"),
        P("segment", "head", None),
        P("segment", "head", None, None),
    )
    return jax.shard_map(
        shards,
        mesh=mesh,
        in_specs=placed,
        out_specs=P("segment", None, "seq", "head"),
        check_vma=False,
    )
```

```python
import functools

import jax
import jax.numpy as jnp
from jax import lax
from jax.experimental import pallas as pl
from jax.experimental.pallas import tpu as pltpu
from jax.sharding import PartitionSpec as P

NS_STEPS = 2

ns_first = 3.4445
ns_second = -4.775
ns_third = 2.0315
update_step = 1.0
norm_eps = 1e-06
grad_eps = 1e-07


def rms_scale(values):
    return values * lax.rsqrt(jnp.mean(values * values, axis=-1, keepdims=True) + norm_eps)


def dot(left, right):
    return jnp.dot(left, right, preferred_element_type=jnp.float32)


def contract(left, right, dims):
    return lax.dot_general(
        left, right, ((dims[:1], dims[1:]), ((), ())), preferred_element_type=jnp.float32
    )


def signal(semaphore, target):
    pl.semaphore_signal(
        semaphore, inc=1, device_id=target, device_id_type=pl.DeviceIdType.MESH
    )


def remote(source, target, send_sem, recv_sem, device):
    return pltpu.make_async_remote_copy(
        src_ref=source,
        dst_ref=target,
        send_sem=send_sem,
        recv_sem=recv_sem,
        device_id=device,
        device_id_type=pl.DeviceIdType.MESH,
    )


def step_kernel(
    segments,
    devices,
    heads,
    chunks,
    stream_hbm,
    in_gain_ref,
    qkv_hbm,
    qk_gain_ref,
    gate_hbm,
    up_hbm,
    down_hbm,
    rate_ref,
    out_gain_ref,
    out_hbm,
    result_ref,
    qkv,
    out_weights,
    wide_init,
    down_init,
    whole,
    scaled,
    sums,
    both,
    queries,
    rights,
    work,
    state,
    wide_norms,
    down_norm,
    terms,
    slots,
    qkv_sems,
    load_sems,
    own_sems,
    spread_sends,
    arrivals,
    far_sends,
    far_recvs,
    near_sends,
    near_recvs,
    term_sends,
    term_recvs,
    hop_sends,
    relay_sends,
    around_sends,
    around_recvs,
    ready,
    *vias,
):
    segment = lax.axis_index("segment")
    place_seq = lax.axis_index("seq")
    me = lax.axis_index("head")
    spans, rows, width = result_ref.shape
    features = whole.shape[2]
    chips = devices // 2
    chip, core = place_seq // 2, lax.rem(place_seq, 2)
    partner = {"seq": 2 * chip + 1 - core}
    piece = rows // chunks
    unit = chunks // 8
    around = 4 * unit if segments > 1 else 0
    via = vias[0] if around else None
    last_segment = segments - 1
    straight = chunks - 1

    loads = [pltpu.make_async_copy(qkv_hbm.at[part], qkv.at[part], qkv_sems.at[part]) for part in range(3)]
    fast_loads = [
        pltpu.make_async_copy(gate_hbm, wide_init.at[0], load_sems.at[0]),
        pltpu.make_async_copy(up_hbm, wide_init.at[1], load_sems.at[1]),
        pltpu.make_async_copy(down_hbm, down_init, load_sems.at[2]),
    ]
    out_load = pltpu.make_async_copy(out_hbm, out_weights, load_sems.at[3])
    for copy in fast_loads:
        copy.start()

    def other_head(step):
        return lax.rem(me + step, heads)

    barrier = pltpu.get_barrier_semaphore()
    for away in range(segments):
        for step in range(heads):
            if away or step:
                signal(barrier, {"segment": lax.rem(segment + away, segments), "head": other_head(step)})
    for step in range(1, chips):
        signal(barrier, {"seq": 2 * lax.rem(chip + step, chips) + core})
    signal(barrier, partner)
    pl.semaphore_wait(barrier, segments * heads - 1 + chips)

    def columns_of(origin):
        return pl.ds(pl.multiple_of(origin * width, width), width)

    def rows_of(chunk):
        if isinstance(chunk, int):
            return pl.ds(chunk * piece, piece)
        return pl.ds(pl.multiple_of(chunk * piece, piece), piece)

    def place(span, origin, chunk):
        return whole.at[span, rows_of(chunk), columns_of(origin)]

    def spread(span, step, chunk):
        return remote(
            stream_hbm.at[span, rows_of(chunk), :],
            place(span, me, chunk),
            spread_sends.at[span, step, chunk],
            arrivals.at[span, me, chunk],
            {"segment": 0, "head": other_head(step)},
        )

    def each_spread(span, action):
        share = chunks // segments

        def one(index, carry):
            for step in range(1, heads):
                action(spread(span, step, segment * share + index))
            return carry

        lax.fori_loop(0, share, one, 0)

    def start(copy):
        copy.start()

    def wait_send(copy):
        copy.wait_send()

    each_spread(0, start)
    for part in (1, 2, 0):
        loads[part].start()
    out_load.start()

    def own_copy(span):
        return pltpu.make_async_copy(
            stream_hbm.at[span], whole.at[span, :, columns_of(me)], own_sems.at[span]
        )

    @pl.when(segment == 0)
    def _():
        for span in range(spans):
            own_copy(span).start()

    for copy in fast_loads:
        copy.wait()
    for index in range(2):
        work[index] = wide_init[index]
        wide = wide_init[index].astype(jnp.float32)
        state[index] = wide
        wide_norms[index] = jnp.sqrt(jnp.sum(wide * wide, axis=0, keepdims=True))
    down = down_init[...].T
    work[2] = down
    down = down.astype(jnp.float32)
    state[2] = down
    down_norm[...] = jnp.sqrt(jnp.sum(down * down, axis=1, keepdims=True))

    def arrival(span, origin, chunk):
        return remote(
            place(span, origin, chunk),
            place(span, origin, chunk),
            hop_sends.at[span, 0, chunk],
            arrivals.at[span, origin, chunk],
            {"head": other_head(1)},
        )

    def relay_copy(span, step, chunk):
        return remote(
            place(span, me, chunk),
            place(span, me, chunk),
            relay_sends.at[span, step, chunk],
            arrivals.at[span, me, chunk],
            {"head": other_head(step)},
        )

    def relay(span, chunk):
        arrival(span, me, chunk).wait_recv()

        @pl.when(chunk < straight)
        def _():
            for step in range(1, heads):
                relay_copy(span, step, chunk).start()

    def project_keys(span):
        sums[0] = jnp.zeros(sums.shape[1:], jnp.float32)
        sums[1] = jnp.zeros(sums.shape[1:], jnp.float32)

        def block(step, squares):
            origin = other_head(step)

            @pl.when(step > 0)
            def _():
                def wait(chunk, carry):
                    arrival(span, origin, chunk).wait_recv()
                    return carry

                lax.fori_loop(0, chunks, wait, 0)

            here = columns_of(origin)
            values = whole[span, :, here].astype(jnp.float32)
            scaled[:, here] = (values * in_gain_ref[:, here]).astype(jnp.bfloat16)
            sums[0] += dot(scaled[:, here], qkv[1, here, :])
            sums[1] += dot(scaled[:, here], qkv[2, here, :])
            return squares + jnp.sum(values * values, axis=1, keepdims=True)

        squares = lax.fori_loop(0, heads, block, jnp.zeros((rows, 1), jnp.float32))
        return lax.rsqrt(squares * (1.0 / features) + norm_eps)

    def rows_at(origin, count=1):
        return pl.ds(pl.multiple_of(origin * rows, rows), count * rows)

    def far_copy(span, part, step):
        return remote(
            both.at[span, part, rows_at(place_seq), :],
            both.at[span, part, rows_at(place_seq), :],
            far_sends.at[span, part, step],
            far_recvs.at[span, part, step],
            {"seq": 2 * lax.rem(chip + step, chips) + core},
        )

    def near_copy(span, part, step):
        origin = 2 * lax.rem(chip + chips - step, chips) + core
        return remote(
            both.at[span, part, rows_at(origin), :],
            both.at[span, part, rows_at(origin), :],
            near_sends.at[span, part, step],
            near_recvs.at[span, part, step],
            partner,
        )

    def project(span):
        scale = project_keys(span)
        own = rows_at(place_seq)
        both[span, 0, own, :] = (rms_scale(sums[0] * scale) * qk_gain_ref[1:2, :]).astype(jnp.bfloat16)
        diagonal = lax.broadcasted_iota(jnp.int32, (rows, rows), 0) == lax.broadcasted_iota(
            jnp.int32, (rows, rows), 1
        )
        rates = jnp.sum(
            jnp.where(diagonal, rate_ref[pl.ds(span, 1), :], 0.0), axis=1, keepdims=True
        )
        both[span, 1, own, :] = (-rates * (sums[1] * scale)).astype(jnp.bfloat16)
        for part in range(2):
            for step in range(1, chips):
                far_copy(span, part, step).start()
        for part in range(2):
            near_copy(span, part, 0).start()
        sums[0] = dot(scaled[...], qkv[0])
        queries[...] = (rms_scale(sums[0] * scale) * qk_gain_ref[0:1, :]).astype(jnp.bfloat16)

    def finish(span, chunk):
        here = rows_of(chunk)
        total = whole[span, here, columns_of(me)].astype(jnp.float32) + terms[
            span, me, here, :
        ].astype(jnp.float32)
        for step in range(1, heads):
            origin = other_head(step)
            term_arrival(span, origin, chunk).wait_recv()
            total += slots[span, origin, here, :].astype(jnp.float32)
        result_ref[span, here, :] = total.astype(jnp.bfloat16)

        @pl.when(segment < last_segment)
        def _():
            hop(span, 0, chunk).start()

            @pl.when(chunk >= straight)
            def _():
                for step in range(1, heads):
                    hop(span, step, chunk).start()

    def term_copy(span, step, chunk):
        target = other_head(step)
        return remote(
            terms.at[span, target, rows_of(chunk), :],
            slots.at[span, me, rows_of(chunk), :],
            term_sends.at[span, step, chunk],
            term_recvs.at[span, me, chunk],
            {"head": target},
        )

    def term_arrival(span, origin, chunk):
        return remote(
            slots.at[span, origin, rows_of(chunk), :],
            slots.at[span, origin, rows_of(chunk), :],
            hop_sends.at[span, 0, chunk],
            term_recvs.at[span, origin, chunk],
            {"head": other_head(1)},
        )

    def hop(span, step, chunk):
        return remote(
            result_ref.at[span, rows_of(chunk), :],
            place(span, me, chunk),
            hop_sends.at[span, step, chunk],
            arrivals.at[span, me, chunk],
            {"segment": segment + 1, "head": other_head(step)},
        )

    def between(span, first, count):
        @pl.when(span > 0)
        def _():
            def one(index, carry):
                finish(span - 1, first + index)
                return carry

            lax.fori_loop(0, count, one, 0)

        @pl.when((segment > 0) & (span + 1 < spans))
        def _():
            def one(index, carry):
                relay(span + 1, first + index)
                return carry

            lax.fori_loop(0, count, one, 0)

    def gradients(span, step):
        for part in range(2):

            @pl.when(step > 0)
            def _():
                remote(
                    both.at[span, part, rows_at(2 * lax.rem(chip + chips - step, chips) + core), :],
                    both.at[span, part, rows_at(2 * lax.rem(chip + chips - step, chips) + core), :],
                    far_sends.at[span, part, step],
                    far_recvs.at[span, part, step],
                    partner,
                ).wait_recv()
                near_copy(span, part, step).start()

        origin = lax.rem(chip + chips - step, chips)
        for part in range(2):
            twin = rows_at(2 * origin + 1 - core)
            remote(
                both.at[span, part, twin, :],
                both.at[span, part, twin, :],
                near_sends.at[span, part, step],
                near_recvs.at[span, part, step],
                partner,
            ).wait_recv()
        here = rows_at(2 * origin, 2)
        keys = both[span, 0, here, :]
        grads = both[span, 1, here, :]
        pre_gate = dot(keys, work[0])
        pre_up = dot(keys, work[1])
        backward = dot(grads, work[2])
        sigmoid_gate = jax.nn.sigmoid(pre_gate)
        gated = pre_gate * sigmoid_gate
        rights[0, here, :] = (
            backward * pre_up * sigmoid_gate * (1.0 + pre_gate * (1.0 - sigmoid_gate))
        ).astype(jnp.bfloat16)
        rights[1, here, :] = (backward * gated).astype(jnp.bfloat16)
        rights[2, here, :] = (gated * pre_up).astype(jnp.bfloat16)

    def orthogonalize(span):
        raw = [contract(both[span, index // 2], rights[index], (0, 0)) for index in range(3)]
        scales = [
            1.0 / (jnp.sqrt(jnp.sum(gradient * gradient, keepdims=True)) + grad_eps)
            for gradient in raw
        ]
        for index in range(3):
            work[index] = (raw[index] * scales[index]).astype(jnp.bfloat16)

        def sweep(step, inner):
            between(span, (3 + step) * unit, unit)
            current = [work[index] for index in range(3)]
            grams = [contract(matrix, matrix, (1, 1)).astype(jnp.bfloat16) for matrix in current]
            squares = [dot(gram, gram) for gram in grams]
            mixings = [
                (ns_second * gram.astype(jnp.float32) + ns_third * square).astype(jnp.bfloat16)
                for gram, square in zip(grams, squares)
            ]
            for index in range(3):
                work[index] = (
                    ns_first * current[index].astype(jnp.float32)
                    + dot(mixings[index], current[index])
                ).astype(jnp.bfloat16)
            return inner

        lax.fori_loop(0, NS_STEPS, sweep, 0)

    def update():
        for index, axis, target in (
            (0, 0, wide_norms[0]),
            (1, 0, wide_norms[1]),
            (2, 1, down_norm[...]),
        ):
            moved = state[index] - update_step * work[index].astype(jnp.float32)
            length = jnp.sqrt(jnp.sum(moved * moved, axis=axis, keepdims=True)) + norm_eps
            fresh = moved * (target / length)
            work[index] = fresh.astype(jnp.bfloat16)
            state[index] = fresh

    def read_out(span):
        gate_out = dot(queries[...], work[0])
        up_out = dot(queries[...], work[1])
        inner = (gate_out * jax.nn.sigmoid(gate_out) * up_out).astype(jnp.bfloat16)
        output = contract(inner, work[2], (1, 1))
        normed_out = (rms_scale(output) * out_gain_ref[...]).astype(jnp.bfloat16)

        for origin in range(heads):
            terms[span, origin] = dot(
                normed_out, out_weights[:, origin * width : (origin + 1) * width]
            ).astype(jnp.bfloat16)
    def detours(span, chunk):
        return (segment == last_segment) & (span == spans - 1) & (chunk >= chunks - around)

    def around_rows(chunk):
        return pl.ds(pl.multiple_of((chunk - (chunks - around)) * piece, piece), piece)

    def around_copy(step, chunk):
        return remote(
            terms.at[spans - 1, other_head(step), rows_of(chunk), :],
            via.at[step, around_rows(chunk), :],
            around_sends.at[step, chunk],
            around_recvs.at[step, chunk],
            {"segment": last_segment - 1},
        )

    def around_arrival(step, chunk):
        return remote(
            via.at[step, around_rows(chunk), :],
            via.at[step, around_rows(chunk), :],
            around_sends.at[step, chunk],
            around_recvs.at[step, chunk],
            {"segment": last_segment},
        )

    def around_onward(step, chunk):
        return remote(
            via.at[step, around_rows(chunk), :],
            slots.at[spans - 1, me, rows_of(chunk), :],
            around_sends.at[step, chunk],
            term_recvs.at[spans - 1, me, chunk],
            {"segment": last_segment, "head": other_head(step)},
        )

    def send_terms(span):
        def send(index, carry):
            chunk = chunks - 1 - index

            @pl.when(detours(span, chunk))
            def _():
                for step in range(1, heads):
                    around_copy(step, chunk).start()

            return carry

        if around:
            lax.fori_loop(0, around, send, 0)

        def send_straight(chunk, carry):
            @pl.when(jnp.logical_not(detours(span, chunk)))
            def _():
                for step in range(1, heads):
                    term_copy(span, step, chunk).start()

            return carry

        lax.fori_loop(0, chunks, send_straight, 0)

    @pl.when(segment == 0)
    def _():
        for span in range(spans):
            own_copy(span).wait()

    @pl.when(segment > 0)
    def _():
        each_spread(0, wait_send)
        for span in range(1, spans):
            pl.semaphore_wait(ready, heads - 1)
            each_spread(span, start)
            each_spread(span, wait_send)

        def one(chunk, carry):
            relay(0, chunk)
            return carry

        lax.fori_loop(0, chunks, one, 0)

    for part in (1, 2, 0):
        loads[part].wait()
    out_load.wait()

    def block(span, carry):
        project(span)

        @pl.when((segment == 0) & (span + 1 < spans))
        def _():
            each_spread(span + 1, start)

            for away in range(1, segments):
                for step in range(1, heads):
                    signal(ready, {"segment": away, "head": other_head(step)})

        def gradient_step(step, inner):
            gradients(span, step)

            @pl.when(step == 0)
            def _():
                between(span, 0, unit)

            return inner

        lax.fori_loop(0, chips, gradient_step, 0)
        between(span, unit, 2 * unit)
        orthogonalize(span)
        between(span, 5 * unit, unit)
        update()
        read_out(span)
        between(span, 6 * unit, 2 * unit)
        send_terms(span)
        return carry

    lax.fori_loop(0, spans, block, 0)

    def last(chunk, carry):
        finish(spans - 1, chunk)
        return carry

    lax.fori_loop(0, chunks, last, 0)

    if around:

        @pl.when(segment == last_segment - 1)
        def _():
            def pass_on(index, carry):
                for step in range(1, heads):
                    around_arrival(step, chunks - 1 - index).wait_recv()
                    around_onward(step, chunks - 1 - index).start()
                return carry

            lax.fori_loop(0, around, pass_on, 0)

            def settle(index, carry):
                for step in range(1, heads):
                    around_onward(step, chunks - 1 - index).wait_send()
                return carry

            lax.fori_loop(0, around, settle, 0)

    @pl.when(segment == 0)
    def _():
        for span in range(spans):
            each_spread(span, wait_send)

    def drain(span, carry):
        def drain_chunk(chunk, inner):
            @pl.when(jnp.logical_not(detours(span, chunk)))
            def _():
                for step in range(1, heads):
                    term_copy(span, step, chunk).wait_send()

            @pl.when(detours(span, chunk))
            def _():
                for step in range(1, heads):
                    around_copy(step, chunk).wait_send()

            @pl.when((segment > 0) & (chunk < straight))
            def _():
                for step in range(1, heads):
                    relay_copy(span, step, chunk).wait_send()

            @pl.when(segment < last_segment)
            def _():
                hop(span, 0, chunk).wait_send()

                @pl.when(chunk >= straight)
                def _():
                    for step in range(1, heads):
                        hop(span, step, chunk).wait_send()

            return inner

        lax.fori_loop(0, chunks, drain_chunk, 0)

        for part in range(2):
            for step in range(1, chips):
                far_copy(span, part, step).wait_send()
            for step in range(chips):
                near_copy(span, part, step).wait_send()
        return carry

    lax.fori_loop(0, spans, drain, 0)


def shards(stream, in_gain, w_qkv, qk_gain, w_one, w_three, w_two, token_rate, out_gain, w_out):
    segments = lax.axis_size("segment")
    devices = lax.axis_size("seq")
    heads = lax.axis_size("head")
    spans, rows, width = stream.shape
    features = w_qkv.shape[1]
    inner, wide = w_one.shape[2:]
    tokens = devices * rows
    chunks = 8
    vmem = pl.BlockSpec(memory_space=pltpu.VMEM)
    anywhere = pl.BlockSpec(memory_space=pl.ANY)
    low = jnp.bfloat16
    dma = pltpu.SemaphoreType.DMA
    result = pl.pallas_call(
        functools.partial(step_kernel, segments, devices, heads, chunks),
        name="step",
        out_shape=jax.ShapeDtypeStruct(stream.shape, low),
        in_specs=[anywhere, vmem, anywhere, vmem, anywhere, anywhere, anywhere, vmem, vmem, anywhere],
        out_specs=vmem,
        scratch_shapes=[
            pltpu.VMEM((3, features, inner), low),
            pltpu.VMEM((inner, features), low),
            pltpu.VMEM((2, inner, wide), low),
            pltpu.VMEM((wide, inner), low),
            pltpu.VMEM((spans, rows, features), low),
            pltpu.VMEM((rows, features), low),
            pltpu.VMEM((2, rows, inner), jnp.float32),
            pltpu.VMEM((spans, 2, tokens, inner), low),
            pltpu.VMEM((rows, inner), low),
            pltpu.VMEM((3, tokens, wide), low),
            pltpu.VMEM((3, inner, wide), low),
            pltpu.VMEM((3, inner, wide), jnp.float32),
            pltpu.VMEM((2, 1, wide), jnp.float32),
            pltpu.VMEM((inner, 1), jnp.float32),
            pltpu.VMEM((spans, heads, rows, width), low),
            pltpu.VMEM((spans, heads, rows, width), low),
            dma((3,)),
            dma((4,)),
            dma((spans,)),
            dma((spans, heads, chunks)),
            dma((spans, heads, chunks)),
            dma((spans, 2, devices // 2)),
            dma((spans, 2, devices // 2)),
            dma((spans, 2, devices // 2)),
            dma((spans, 2, devices // 2)),
            dma((spans, heads, chunks)),
            dma((spans, heads, chunks)),
            dma((spans, heads, chunks)),
            dma((spans, heads, chunks)),
            dma((heads, chunks)),
            dma((heads, chunks)),
            pltpu.SemaphoreType.REGULAR,
        ]
        + ([pltpu.VMEM((heads, 4 * (chunks // 8) * (rows // chunks), width), low)] if segments > 1 else []),
        compiler_params=pltpu.CompilerParams(
            collective_id=0, has_side_effects=True, vmem_limit_bytes=67043328
        ),
    )(
        stream,
        in_gain,
        jnp.transpose(w_qkv[0, :, 0], (1, 0, 2)),
        qk_gain[0, 0],
        w_one[0, 0],
        w_three[0, 0],
        w_two[0, 0],
        token_rate[0],
        out_gain[0, :1],
        w_out[0, 0],
    )
    return result[None]


def solution(mesh):
    placed = (
        P(None, "seq", "head"),
        P("segment", None),
        P("segment", None, "head", None, None),
        P("segment", "head", None, None),
        P("segment", "head", None, None),
        P("segment", "head", None, None),
        P("segment", "head", None, None),
        P("segment", None, "seq"),
        P("segment", "head", None),
        P("segment", "head", None, None),
    )
    return jax.shard_map(
        shards,
        mesh=mesh,
        in_specs=placed,
        out_specs=P("segment", None, "seq", "head"),
        check_vma=False,
    )
```

```python
import functools

import jax
import jax.numpy as jnp
from jax import lax
from jax.experimental import pallas as pl
from jax.experimental.pallas import tpu as pltpu
from jax.sharding import PartitionSpec as P

NS_STEPS = 2

ns_first = 3.4445
ns_second = -4.775
ns_third = 2.0315
update_step = 1.0
norm_eps = 1e-06
grad_eps = 1e-07


def rms_scale(values):
    return values * lax.rsqrt(jnp.mean(values * values, axis=-1, keepdims=True) + norm_eps)


def dot(left, right):
    return jnp.dot(left, right, preferred_element_type=jnp.float32)


def contract(left, right, dims):
    return lax.dot_general(
        left, right, ((dims[:1], dims[1:]), ((), ())), preferred_element_type=jnp.float32
    )


def signal(semaphore, target):
    pl.semaphore_signal(
        semaphore, inc=1, device_id=target, device_id_type=pl.DeviceIdType.MESH
    )


def remote(source, target, send_sem, recv_sem, device):
    return pltpu.make_async_remote_copy(
        src_ref=source,
        dst_ref=target,
        send_sem=send_sem,
        recv_sem=recv_sem,
        device_id=device,
        device_id_type=pl.DeviceIdType.MESH,
    )


def step_kernel(
    segments,
    devices,
    heads,
    chunks,
    stream_hbm,
    in_gain_ref,
    qkv_hbm,
    qk_gain_ref,
    gate_hbm,
    up_hbm,
    down_hbm,
    rate_ref,
    out_gain_ref,
    out_hbm,
    result_ref,
    qkv,
    out_weights,
    wide_init,
    down_init,
    whole,
    scaled,
    row_scale,
    sums,
    both,
    queries,
    rights,
    work,
    state,
    wide_norms,
    down_norm,
    terms,
    slots,
    qkv_sems,
    load_sems,
    own_sems,
    spread_sends,
    arrivals,
    own_recvs,
    pass_recvs,
    far_sends,
    far_recvs,
    near_sends,
    near_recvs,
    term_sends,
    term_recvs,
    hop_sends,
    straight_sends,
    relay_sends,
    around_sends,
    around_recvs,
    ready,
    pass_sends,
    aside_sends,
    aside_recvs,
    aside,
    *vias,
):
    segment = lax.axis_index("segment")
    place_seq = lax.axis_index("seq")
    me = lax.axis_index("head")
    spans, rows, width = result_ref.shape
    features = whole.shape[2]
    chips = devices // 2
    chip, core = place_seq // 2, lax.rem(place_seq, 2)
    partner = {"seq": 2 * chip + 1 - core}
    piece = rows // chunks
    unit = chunks // 8
    around = 3 * unit if segments > 1 else 0
    via = vias[0] if around else None
    last_segment = segments - 1

    loads = [pltpu.make_async_copy(qkv_hbm.at[part], qkv.at[part], qkv_sems.at[part]) for part in range(3)]
    fast_loads = [
        pltpu.make_async_copy(gate_hbm, wide_init.at[0], load_sems.at[0]),
        pltpu.make_async_copy(up_hbm, wide_init.at[1], load_sems.at[1]),
        pltpu.make_async_copy(down_hbm, down_init, load_sems.at[2]),
    ]
    out_load = pltpu.make_async_copy(out_hbm, out_weights, load_sems.at[3])
    for copy in fast_loads:
        copy.start()

    def other_head(step):
        up, down = step - 1, heads - step
        upward = jnp.where(up >= me, up + 1, up)
        downward = jnp.where(down > me, down, down - 1)
        return jnp.where(2 * me < heads, downward, upward)

    barrier = pltpu.get_barrier_semaphore()
    for away in range(segments):
        for step in range(heads):
            if away or step:
                signal(
                    barrier,
                    {"segment": lax.rem(segment + away, segments), "head": lax.rem(me + step, heads)},
                )
    for step in range(1, chips):
        signal(barrier, {"seq": 2 * lax.rem(chip + step, chips) + core})
    signal(barrier, partner)
    pl.semaphore_wait(barrier, segments * heads - 1 + chips)

    def columns_of(origin):
        return pl.ds(pl.multiple_of(origin * width, width), width)

    def rows_of(chunk):
        if isinstance(chunk, int):
            return pl.ds(chunk * piece, piece)
        return pl.ds(pl.multiple_of(chunk * piece, piece), piece)

    def place(span, origin, chunk):
        return whole.at[span, rows_of(chunk), columns_of(origin)]

    def await_arrival(like, semaphore):
        remote(like, like, semaphore, semaphore, partner).wait_recv()

    def await_sent(like, semaphore):
        remote(like, like, semaphore, semaphore, partner).wait_send()

    def as_many(blocks, count):
        return terms.at[0, pl.ds(0, blocks), pl.ds(0, count * piece), :]

    def spread(span, step, chunk):
        return remote(
            stream_hbm.at[span, rows_of(chunk), :],
            place(span, me, chunk),
            spread_sends.at[span],
            arrivals.at[span, me],
            {"segment": 0, "head": other_head(step)},
        )

    share = chunks // segments

    def start_spread(span):
        def one(index, carry):
            for step in range(1, heads):
                spread(span, step, segment * share + index).start()
            return carry

        lax.fori_loop(0, share, one, 0)

    def settle_spread(span):
        await_sent(as_many(heads - 1, share), spread_sends.at[span])

    start_spread(0)
    for part in (1, 2, 0):
        loads[part].start()
    out_load.start()

    def own_copy(span):
        return pltpu.make_async_copy(
            stream_hbm.at[span], whole.at[span, :, columns_of(me)], own_sems.at[span]
        )

    @pl.when(segment == 0)
    def _():
        for span in range(spans):
            own_copy(span).start()

    for copy in fast_loads:
        copy.wait()
    for index in range(2):
        work[index] = wide_init[index]
        wide = wide_init[index].astype(jnp.float32)
        state[index] = wide
        wide_norms[index] = jnp.sqrt(jnp.sum(wide * wide, axis=0, keepdims=True))
    down = down_init[...].T
    work[2] = down
    down = down.astype(jnp.float32)
    state[2] = down
    down_norm[...] = jnp.sqrt(jnp.sum(down * down, axis=1, keepdims=True))

    def goes_straight(span, chunk):
        return (span > 0) & (chunk >= chunks - 2 * unit)

    def relay_copy(span, step, chunk):
        return remote(
            place(span, me, chunk),
            place(span, me, chunk),
            relay_sends.at[span],
            arrivals.at[span, me],
            {"head": other_head(step)},
        )

    def passing(side, origin, chunk):
        return remote(
            place(0, origin, chunk),
            place(0, origin, chunk),
            pass_sends.at[side, origin],
            pass_recvs.at[origin, chunk],
            {"head": me + 1 - 2 * side},
        )

    has_next = (me + 1 < heads, me >= 1)
    passed_on = chunks - unit

    def each_passing(side, distance, chunk, action):
        origin = me - distance * (1 - 2 * side)

        @pl.when(
            (chunk >= 0) & (chunk < passed_on) & (origin >= 0) & (origin < heads) & has_next[side]
        )
        def _():
            action(side, origin, chunk)

    def pass_first_block():
        def forward(side, origin, chunk):
            await_arrival(place(0, origin, chunk), pass_recvs.at[origin, chunk])
            passing(side, origin, chunk).start()

        def moment(now, carry):
            @pl.when(now < passed_on)
            def _():
                await_arrival(place(0, me, now), own_recvs.at[0, now])

            @pl.when((now >= passed_on) & (now < chunks))
            def _():
                relay(0, now)

            for side in range(2):
                each_passing(side, 0, now, lambda *which: passing(*which).start())
            for distance in range(1, heads - 1):
                for side in range(2):
                    each_passing(side, distance, now - distance, forward)
            return carry

        lax.fori_loop(0, chunks + heads - 2, moment, 0)

    def settle_first_block():
        def settle_passing(side, origin, chunk):
            await_sent(as_many(1, passed_on), pass_sends.at[side, origin])

        for distance in range(heads - 1):
            for side in range(2):
                each_passing(side, distance, 0, settle_passing)

    def relay(span, chunk):
        await_arrival(place(span, me, chunk), own_recvs.at[span, chunk])

        @pl.when(jnp.logical_not(goes_straight(span, chunk)))
        def _():
            for step in range(1, heads):
                relay_copy(span, step, chunk).start()

    def project_keys(span):
        sums[0] = jnp.zeros(sums.shape[1:], jnp.float32)
        sums[1] = jnp.zeros(sums.shape[1:], jnp.float32)

        def block(step, squares):
            origin = lax.rem(me + step, heads)

            first = (segment > 0) & (span == 0)
            passed = jnp.where(origin < me, me + 1 < heads, me >= 1)

            @pl.when((step > 0) & jnp.logical_not(first))
            def _():
                await_arrival(whole.at[span, :, columns_of(origin)], arrivals.at[span, origin])

            @pl.when((step > 0) & first)
            def _():
                await_arrival(place(span, origin, passed_on), arrivals.at[span, origin])

            @pl.when((step > 0) & first & jnp.logical_not(passed))
            def _():
                def wait(chunk, carry):
                    await_arrival(place(span, origin, chunk), pass_recvs.at[origin, chunk])
                    return carry

                lax.fori_loop(0, passed_on, wait, 0)

            here = columns_of(origin)
            values = whole[span, :, here].astype(jnp.float32)
            scaled[:, here] = (values * in_gain_ref[:, here]).astype(jnp.bfloat16)
            sums[0] += dot(scaled[:, here], qkv[1, here, :])
            sums[1] += dot(scaled[:, here], qkv[2, here, :])
            return squares + jnp.sum(values * values, axis=1, keepdims=True)

        squares = lax.fori_loop(0, heads, block, jnp.zeros((rows, 1), jnp.float32))
        row_scale[...] = lax.rsqrt(squares * (1.0 / features) + norm_eps)

    def rows_at(origin, count=1):
        return pl.ds(pl.multiple_of(origin * rows, rows), count * rows)

    def far_copy(span, part, step):
        return remote(
            both.at[span, part, rows_at(place_seq), :],
            both.at[span, part, rows_at(place_seq), :],
            far_sends.at[span],
            far_recvs.at[span, part, step],
            {"seq": 2 * lax.rem(chip + step, chips) + core},
        )

    def near_copy(span, part, step):
        origin = 2 * lax.rem(chip + chips - step, chips) + core
        return remote(
            both.at[span, part, rows_at(origin), :],
            both.at[span, part, rows_at(origin), :],
            near_sends.at[span],
            near_recvs.at[span, step],
            partner,
        )

    def project_pair(span):
        project_keys(span)
        scale = row_scale[...]
        own = rows_at(place_seq)
        both[span, 0, own, :] = (rms_scale(sums[0] * scale) * qk_gain_ref[1:2, :]).astype(jnp.bfloat16)
        diagonal = lax.broadcasted_iota(jnp.int32, (rows, rows), 0) == lax.broadcasted_iota(
            jnp.int32, (rows, rows), 1
        )
        rates = jnp.sum(
            jnp.where(diagonal, rate_ref[pl.ds(span, 1), :], 0.0), axis=1, keepdims=True
        )
        both[span, 1, own, :] = (-rates * (sums[1] * scale)).astype(jnp.bfloat16)
        for part in range(2):
            for step in range(1, chips):
                far_copy(span, part, step).start()
        for part in range(2):
            near_copy(span, part, 0).start()

    def project_queries():
        queries[...] = (rms_scale(dot(scaled[...], qkv[0]) * row_scale[...]) * qk_gain_ref[0:1, :]).astype(jnp.bfloat16)

    def finish(span, chunk):
        here = rows_of(chunk)
        total = whole[span, here, columns_of(me)].astype(jnp.float32) + terms[
            span, me, here, :
        ].astype(jnp.float32)
        await_arrival(as_many(heads - 1, 1), term_recvs.at[span, chunk])
        for step in range(1, heads):
            origin = other_head(step)
            total += slots[span, origin, here, :].astype(jnp.float32)
        result_ref[span, here, :] = total.astype(jnp.bfloat16)

        @pl.when(segment < last_segment)
        def _():
            hop(span, 0, chunk).start()

            @pl.when(goes_straight(span, chunk))
            def _():
                for step in range(1, heads):
                    hop(span, step, chunk).start()

    def term_copy(span, step, chunk):
        target = other_head(step)
        return remote(
            terms.at[span, target, rows_of(chunk), :],
            slots.at[span, me, rows_of(chunk), :],
            term_sends.at[span],
            term_recvs.at[span, chunk],
            {"head": target},
        )

    def hop(span, step, chunk):
        return remote(
            result_ref.at[span, rows_of(chunk), :],
            place(span, me, chunk),
            straight_sends.at[span] if step else hop_sends.at[span],
            arrivals.at[span, me] if step else own_recvs.at[span, chunk],
            {"segment": segment + 1, "head": other_head(step) if step else me},
        )

    def finish_some(span, first, count):
        @pl.when((segment < last_segment) & (span > 0))
        def _():
            def one(index, carry):
                finish(span - 1, first + index)
                return carry

            lax.fori_loop(0, count, one, 0)

    def relay_some(span, first, count):
        @pl.when((segment > 0) & (span + 1 < spans))
        def _():
            def one(index, carry):
                relay(span + 1, first + index)
                return carry

            lax.fori_loop(0, count, one, 0)

    def gradients(span, step):
        for part in range(2):

            @pl.when(step > 0)
            def _():
                there = rows_at(2 * lax.rem(chip + chips - step, chips) + core)
                await_arrival(both.at[span, part, there, :], far_recvs.at[span, part, step])
                near_copy(span, part, step).start()

        origin = lax.rem(chip + chips - step, chips)
        await_arrival(
            both.at[span, :, rows_at(2 * origin + 1 - core), :], near_recvs.at[span, step]
        )
        here = rows_at(2 * origin, 2)
        keys = both[span, 0, here, :]
        grads = both[span, 1, here, :]
        pre_gate = dot(keys, work[0])
        pre_up = dot(keys, work[1])
        backward = dot(grads, work[2])
        sigmoid_gate = jax.nn.sigmoid(pre_gate)
        gated = pre_gate * sigmoid_gate
        rights[0, here, :] = (
            backward * pre_up * sigmoid_gate * (1.0 + pre_gate * (1.0 - sigmoid_gate))
        ).astype(jnp.bfloat16)
        rights[1, here, :] = (backward * gated).astype(jnp.bfloat16)
        rights[2, here, :] = (gated * pre_up).astype(jnp.bfloat16)

    def orthogonalize(span):
        raw = [contract(both[span, index // 2], rights[index], (0, 0)) for index in range(3)]
        scales = [
            1.0 / (jnp.sqrt(jnp.sum(gradient * gradient, keepdims=True)) + grad_eps)
            for gradient in raw
        ]
        for index in range(3):
            work[index] = (raw[index] * scales[index]).astype(jnp.bfloat16)

        def sweep(step, inner):
            finish_some(span, (2 + step) * unit, (1 + step) * unit)
            relay_some(span, (3 + step) * unit, (1 + step) * unit)
            current = [work[index] for index in range(3)]
            grams = [contract(matrix, matrix, (1, 1)).astype(jnp.bfloat16) for matrix in current]
            squares = [dot(gram, gram) for gram in grams]
            mixings = [
                (ns_second * gram.astype(jnp.float32) + ns_third * square).astype(jnp.bfloat16)
                for gram, square in zip(grams, squares)
            ]
            for index in range(3):
                work[index] = (
                    ns_first * current[index].astype(jnp.float32)
                    + dot(mixings[index], current[index])
                ).astype(jnp.bfloat16)
            return inner

        lax.fori_loop(0, NS_STEPS, sweep, 0)

    def update():
        for index, axis, target in (
            (0, 0, wide_norms[0]),
            (1, 0, wide_norms[1]),
            (2, 1, down_norm[...]),
        ):
            moved = state[index] - update_step * work[index].astype(jnp.float32)
            length = jnp.sqrt(jnp.sum(moved * moved, axis=axis, keepdims=True)) + norm_eps
            fresh = moved * (target / length)
            work[index] = fresh.astype(jnp.bfloat16)
            state[index] = fresh

    def read_out(span):
        gate_out = dot(queries[...], work[0])
        up_out = dot(queries[...], work[1])
        inner = (gate_out * jax.nn.sigmoid(gate_out) * up_out).astype(jnp.bfloat16)
        output = contract(inner, work[2], (1, 1))
        normed_out = (rms_scale(output) * out_gain_ref[...]).astype(jnp.bfloat16)

        for origin in range(heads):
            terms[span, origin] = dot(
                normed_out, out_weights[:, origin * width : (origin + 1) * width]
            ).astype(jnp.bfloat16)
    def detours(span, chunk):
        return (segment == last_segment) & (chunk >= chunks - around)

    def steps_aside(span, chunk):
        if segments == 1:
            return segment < 0
        return (segment == 0) & (span == 0) & ((chunk // unit == 2) | (chunk // unit == 4))

    def aside_chunk(place_at):
        return (2 + 2 * (place_at // unit)) * unit + lax.rem(place_at, unit)

    def aside_rows(place_at):
        return pl.ds(pl.multiple_of(place_at * piece, piece), piece)

    def aside_copy(step, place_at):
        return remote(
            terms.at[0, other_head(step), rows_of(aside_chunk(place_at)), :],
            aside.at[step, aside_rows(place_at), :],
            aside_sends.at[0],
            aside_recvs.at[place_at],
            {"segment": 1},
        )

    def aside_onward(step, place_at):
        return remote(
            aside.at[step, aside_rows(place_at), :],
            slots.at[0, me, rows_of(aside_chunk(place_at)), :],
            aside_sends.at[0],
            term_recvs.at[0, aside_chunk(place_at)],
            {"segment": 0, "head": other_head(step)},
        )

    def each_aside(action):
        def one(place_at, carry):
            for step in range(1, heads):
                action(step, place_at).start()
            return carry

        lax.fori_loop(0, 2 * unit, one, 0)

    def pass_aside():
        def one(place_at, carry):
            await_arrival(as_many(heads - 1, 1), aside_recvs.at[place_at])
            for step in range(1, heads):
                aside_onward(step, place_at).start()
            return carry

        lax.fori_loop(0, 2 * unit, one, 0)

    def settle_aside():
        await_sent(as_many(heads - 1, 2 * unit), aside_sends.at[0])

    def around_rows(chunk):
        return pl.ds(pl.multiple_of((chunk - (chunks - around)) * piece, piece), piece)

    def around_copy(span, step, chunk):
        return remote(
            terms.at[span, other_head(step), rows_of(chunk), :],
            via.at[span, step, around_rows(chunk), :],
            around_sends.at[span],
            around_recvs.at[span, chunk - (chunks - around)],
            {"segment": last_segment - 1},
        )

    def around_onward(span, step, chunk):
        return remote(
            via.at[span, step, around_rows(chunk), :],
            slots.at[span, me, rows_of(chunk), :],
            around_sends.at[span],
            term_recvs.at[span, chunk],
            {"segment": last_segment, "head": other_head(step)},
        )

    def send_terms(span):
        def send(index, carry):
            chunk = chunks - 1 - index

            @pl.when(detours(span, chunk))
            def _():
                for step in range(1, heads):
                    around_copy(span, step, chunk).start()

            return carry

        if around:
            lax.fori_loop(0, around, send, 0)

            @pl.when((segment == 0) & (span == 0))
            def _():
                each_aside(aside_copy)

        def send_straight(chunk, carry):
            @pl.when(jnp.logical_not(detours(span, chunk) | steps_aside(span, chunk)))
            def _():
                for step in range(1, heads):
                    term_copy(span, step, chunk).start()

            return carry

        lax.fori_loop(0, chunks, send_straight, 0)

    @pl.when(segment == 0)
    def _():
        for span in range(spans):
            own_copy(span).wait()

    @pl.when(segment > 0)
    def _():
        settle_spread(0)
        for span in range(1, spans):
            pl.semaphore_wait(ready, heads - 1)
            start_spread(span)
            settle_spread(span)

        @pl.when(segment == 1)
        def _():
            pass_aside()

        pass_first_block()

    for part in (1, 2, 0):
        loads[part].wait()
    out_load.wait()

    def block(span, carry):
        @pl.when((segment > 0) | (span == 0))
        def _():
            project_pair(span)

        @pl.when((segment == last_segment) & (span > 0))
        def _():
            send_terms(span - 1)

        @pl.when((segment == 0) & (span + 1 < spans))
        def _():
            start_spread(span + 1)

            for away in range(1, segments):
                for step in range(1, heads):
                    signal(ready, {"segment": away, "head": other_head(step)})

        relay_some(span, 0, unit)
        project_queries()

        def gradient_step(step, inner):
            gradients(span, step)

            @pl.when(step == 0)
            def _():
                finish_some(span, 0, unit)
                relay_some(span, unit, unit)

            return inner

        lax.fori_loop(0, chips, gradient_step, 0)
        finish_some(span, unit, unit)
        relay_some(span, 2 * unit, unit)
        orthogonalize(span)
        finish_some(span, 5 * unit, 2 * unit)

        @pl.when((segment == 0) & (span + 1 < spans))
        def _():
            project_pair(span + 1)

        update()
        read_out(span)
        finish_some(span, 7 * unit, unit)
        relay_some(span, 6 * unit, 2 * unit)

        @pl.when((segment < last_segment) | (span == spans - 1))
        def _():
            send_terms(span)

        return carry

    lax.fori_loop(0, spans, block, 0)

    @pl.when(segment == 0)
    def _():
        for span in range(spans):
            settle_spread(span)
        if segments > 1:
            settle_aside()

    @pl.when(segment > 0)
    def _():
        settle_first_block()
        await_sent(as_many(heads - 1, unit), relay_sends.at[0])
        for span in range(1, spans):
            await_sent(as_many(heads - 1, chunks - 2 * unit), relay_sends.at[span])

        @pl.when(segment == 1)
        def _():
            settle_aside()

    def settle_terms(span):
        beside = 2 * unit if segments > 1 and span == 0 else 0

        @pl.when((segment > 0) & (segment < last_segment))
        def _():
            await_sent(as_many(heads - 1, chunks), term_sends.at[span])

        @pl.when((segment == 0) & (segment < last_segment))
        def _():
            await_sent(as_many(heads - 1, chunks - beside), term_sends.at[span])

        @pl.when(segment == last_segment)
        def _():
            await_sent(as_many(heads - 1, chunks - around), term_sends.at[span])
            if around:
                await_sent(as_many(heads - 1, around), around_sends.at[span])

    def settle_hops(span):
        @pl.when(segment < last_segment)
        def _():
            await_sent(as_many(1, chunks), hop_sends.at[span])
            if span:
                await_sent(as_many(heads - 1, 2 * unit), straight_sends.at[span])

    for span in range(spans):
        if span + 1 < spans:
            settle_terms(span)
            settle_hops(span)
        if chips > 1:
            await_sent(both.at[span, :, pl.ds(0, (chips - 1) * rows), :], far_sends.at[span])
        await_sent(both.at[span, :, pl.ds(0, chips * rows), :], near_sends.at[span])

    def last(index, carry):
        finish(index // chunks, lax.rem(index, chunks))
        return carry

    lax.fori_loop(jnp.where(segment < last_segment, (spans - 1) * chunks, 0), spans * chunks, last, 0)

    if around:

        @pl.when(segment == last_segment - 1)
        def _():
            def pass_on(index, carry):
                span, chunk = index // around, chunks - 1 - lax.rem(index, around)
                await_arrival(
                    as_many(heads - 1, 1), around_recvs.at[span, chunk - (chunks - around)]
                )
                for step in range(1, heads):
                    around_onward(span, step, chunk).start()
                return carry

            lax.fori_loop(0, spans * around, pass_on, 0)
            for span in range(spans):
                await_sent(as_many(heads - 1, around), around_sends.at[span])

    settle_terms(spans - 1)
    settle_hops(spans - 1)


def shards(stream, in_gain, w_qkv, qk_gain, w_one, w_three, w_two, token_rate, out_gain, w_out):
    segments = lax.axis_size("segment")
    devices = lax.axis_size("seq")
    heads = lax.axis_size("head")
    spans, rows, width = stream.shape
    features = w_qkv.shape[1]
    inner, wide = w_one.shape[2:]
    tokens = devices * rows
    chunks = 8
    vmem = pl.BlockSpec(memory_space=pltpu.VMEM)
    anywhere = pl.BlockSpec(memory_space=pl.ANY)
    low = jnp.bfloat16
    dma = pltpu.SemaphoreType.DMA
    result = pl.pallas_call(
        functools.partial(step_kernel, segments, devices, heads, chunks),
        name="step",
        out_shape=jax.ShapeDtypeStruct(stream.shape, low),
        in_specs=[anywhere, vmem, anywhere, vmem, anywhere, anywhere, anywhere, vmem, vmem, anywhere],
        out_specs=vmem,
        scratch_shapes=[
            pltpu.VMEM((3, features, inner), low),
            pltpu.VMEM((inner, features), low),
            pltpu.VMEM((2, inner, wide), low),
            pltpu.VMEM((wide, inner), low),
            pltpu.VMEM((spans, rows, features), low),
            pltpu.VMEM((rows, features), low),
            pltpu.VMEM((rows, 1), jnp.float32),
            pltpu.VMEM((2, rows, inner), jnp.float32),
            pltpu.VMEM((spans, 2, tokens, inner), low),
            pltpu.VMEM((rows, inner), low),
            pltpu.VMEM((3, tokens, wide), low),
            pltpu.VMEM((3, inner, wide), low),
            pltpu.VMEM((3, inner, wide), jnp.float32),
            pltpu.VMEM((2, 1, wide), jnp.float32),
            pltpu.VMEM((inner, 1), jnp.float32),
            pltpu.VMEM((spans, heads, rows, width), low),
            pltpu.VMEM((spans, heads, rows, width), low),
            dma((3,)),
            dma((4,)),
            dma((spans,)),
            dma((spans,)),
            dma((spans, heads)),
            dma((spans, chunks)),
            dma((heads, chunks)),
            dma((spans,)),
            dma((spans, 2, devices // 2)),
            dma((spans,)),
            dma((spans, devices // 2)),
            dma((spans,)),
            dma((spans, chunks)),
            dma((spans,)),
            dma((spans,)),
            dma((spans,)),
            dma((spans,)),
            dma((spans, 3 * (chunks // 8))),
            pltpu.SemaphoreType.REGULAR,
            dma((2, heads)),
            dma((1,)),
            dma((chunks // 4,)),
            pltpu.VMEM((heads, rows // 4, width), low),
        ]
        + ([pltpu.VMEM((spans, heads, 3 * (chunks // 8) * (rows // chunks), width), low)] if segments > 1 else []),
        compiler_params=pltpu.CompilerParams(
            collective_id=0, has_side_effects=True, vmem_limit_bytes=67043328
        ),
    )(
        stream,
        in_gain,
        jnp.transpose(w_qkv[0, :, 0], (1, 0, 2)),
        qk_gain[0, 0],
        w_one[0, 0],
        w_three[0, 0],
        w_two[0, 0],
        token_rate[0],
        out_gain[0, :1],
        w_out[0, 0],
    )
    return result[None]


def solution(mesh):
    placed = (
        P(None, "seq", "head"),
        P("segment", None),
        P("segment", None, "head", None, None),
        P("segment", "head", None, None),
        P("segment", "head", None, None),
        P("segment", "head", None, None),
        P("segment", "head", None, None),
        P("segment", None, "seq"),
        P("segment", "head", None),
        P("segment", "head", None, None),
    )
    return jax.shard_map(
        shards,
        mesh=mesh,
        in_specs=placed,
        out_specs=P("segment", None, "seq", "head"),
        check_vma=False,
    )
```

```python
import functools

import jax
import jax.numpy as jnp
from jax import lax
from jax.experimental import pallas as pl
from jax.experimental.pallas import tpu as pltpu
from jax.sharding import PartitionSpec as P

NS_STEPS = 2

ns_first = 3.4445
ns_second = -4.775
ns_third = 2.0315
update_step = 1.0
norm_eps = 1e-06
grad_eps = 1e-07


def rms_scale(values):
    return values * lax.rsqrt(jnp.mean(values * values, axis=-1, keepdims=True) + norm_eps)


def dot(left, right):
    return jnp.dot(left, right, preferred_element_type=jnp.float32)


def contract(left, right, dims):
    return lax.dot_general(
        left, right, ((dims[:1], dims[1:]), ((), ())), preferred_element_type=jnp.float32
    )


def signal(semaphore, target):
    pl.semaphore_signal(
        semaphore, inc=1, device_id=target, device_id_type=pl.DeviceIdType.MESH
    )


def remote(source, target, send_sem, recv_sem, device):
    return pltpu.make_async_remote_copy(
        src_ref=source,
        dst_ref=target,
        send_sem=send_sem,
        recv_sem=recv_sem,
        device_id=device,
        device_id_type=pl.DeviceIdType.MESH,
    )


def step_kernel(
    segments,
    devices,
    heads,
    chunks,
    stream_hbm,
    in_gain_ref,
    qkv_hbm,
    qk_gain_ref,
    gate_hbm,
    up_hbm,
    down_hbm,
    rate_ref,
    out_gain_ref,
    out_hbm,
    result_ref,
    qkv,
    out_weights,
    wide_init,
    down_init,
    whole,
    scaled,
    row_scale,
    sums,
    both,
    queries,
    rights,
    work,
    state,
    wide_norms,
    down_norm,
    terms,
    slots,
    qkv_sems,
    load_sems,
    own_sems,
    spread_sends,
    arrivals,
    own_recvs,
    pass_recvs,
    far_sends,
    far_recvs,
    near_sends,
    near_recvs,
    term_sends,
    term_recvs,
    hop_sends,
    straight_sends,
    relay_sends,
    around_sends,
    around_recvs,
    ready,
    pass_sends,
    aside_sends,
    aside_recvs,
    aside,
    *vias,
):
    segment = lax.axis_index("segment")
    place_seq = lax.axis_index("seq")
    me = lax.axis_index("head")
    spans, rows, width = result_ref.shape
    features = whole.shape[2]
    chips = devices // 2
    chip, core = place_seq // 2, lax.rem(place_seq, 2)
    partner = {"seq": 2 * chip + 1 - core}
    piece = rows // chunks
    unit = chunks // 8
    around = 3 * unit if segments > 1 else 0
    via = vias[0] if around else None
    last_segment = segments - 1

    loads = [pltpu.make_async_copy(qkv_hbm.at[part], qkv.at[part], qkv_sems.at[part]) for part in range(3)]
    fast_loads = [
        pltpu.make_async_copy(gate_hbm, wide_init.at[0], load_sems.at[0]),
        pltpu.make_async_copy(up_hbm, wide_init.at[1], load_sems.at[1]),
        pltpu.make_async_copy(down_hbm, down_init, load_sems.at[2]),
    ]
    out_load = pltpu.make_async_copy(out_hbm, out_weights, load_sems.at[3])
    for copy in fast_loads:
        copy.start()

    def other_head(step):
        up, down = step - 1, heads - step
        upward = jnp.where(up >= me, up + 1, up)
        downward = jnp.where(down > me, down, down - 1)
        return jnp.where(2 * me < heads, downward, upward)

    barrier = pltpu.get_barrier_semaphore()
    for away in range(segments):
        for step in range(heads):
            if away or step:
                signal(
                    barrier,
                    {"segment": lax.rem(segment + away, segments), "head": lax.rem(me + step, heads)},
                )
    for step in range(1, chips):
        signal(barrier, {"seq": 2 * lax.rem(chip + step, chips) + core})
    signal(barrier, partner)
    pl.semaphore_wait(barrier, segments * heads - 1 + chips)

    def columns_of(origin):
        return pl.ds(pl.multiple_of(origin * width, width), width)

    def rows_of(chunk):
        if isinstance(chunk, int):
            return pl.ds(chunk * piece, piece)
        return pl.ds(pl.multiple_of(chunk * piece, piece), piece)

    def place(span, origin, chunk):
        return whole.at[span, rows_of(chunk), columns_of(origin)]

    def await_arrival(like, semaphore):
        remote(like, like, semaphore, semaphore, partner).wait_recv()

    def await_sent(like, semaphore):
        remote(like, like, semaphore, semaphore, partner).wait_send()

    def as_many(blocks, count):
        return terms.at[0, pl.ds(0, blocks), pl.ds(0, count * piece), :]

    def spread(span, step, chunk):
        return remote(
            stream_hbm.at[span, rows_of(chunk), :],
            place(span, me, chunk),
            spread_sends.at[span],
            arrivals.at[span, me],
            {"segment": 0, "head": other_head(step)},
        )

    share = chunks // segments

    def start_spread(span):
        def one(index, carry):
            for step in range(1, heads):
                spread(span, step, segment * share + index).start()
            return carry

        lax.fori_loop(0, share, one, 0)

    def settle_spread(span):
        await_sent(as_many(heads - 1, share), spread_sends.at[span])

    start_spread(0)
    for part in (1, 2, 0):
        loads[part].start()
    out_load.start()

    def own_copy(span):
        return pltpu.make_async_copy(
            stream_hbm.at[span], whole.at[span, :, columns_of(me)], own_sems.at[span]
        )

    @pl.when(segment == 0)
    def _():
        for span in range(spans):
            own_copy(span).start()

    for copy in fast_loads:
        copy.wait()
    for index in range(2):
        work[index] = wide_init[index]
        wide = wide_init[index].astype(jnp.float32)
        state[index] = wide
        wide_norms[index] = jnp.sqrt(jnp.sum(wide * wide, axis=0, keepdims=True))
    down = down_init[...].T
    work[2] = down
    down = down.astype(jnp.float32)
    state[2] = down
    down_norm[...] = jnp.sqrt(jnp.sum(down * down, axis=1, keepdims=True))

    def goes_straight(span, chunk):
        return chunk >= chunks - jnp.where(span > 0, 2 * unit, unit)

    def relay_copy(span, step, chunk):
        return remote(
            place(span, me, chunk),
            place(span, me, chunk),
            relay_sends.at[span],
            arrivals.at[span, me],
            {"head": other_head(step)},
        )

    def passing(side, origin, chunk):
        return remote(
            place(0, origin, chunk),
            place(0, origin, chunk),
            pass_sends.at[side, origin],
            pass_recvs.at[origin, chunk],
            {"head": me + 1 - 2 * side},
        )

    has_next = (me + 1 < heads, me >= 1)
    passed_on = chunks - 5 * unit

    def each_passing(side, distance, chunk, action):
        origin = me - distance * (1 - 2 * side)

        @pl.when(
            (chunk >= 0) & (chunk < passed_on) & (origin >= 0) & (origin < heads) & has_next[side]
        )
        def _():
            action(side, origin, chunk)

    def pass_first_block():
        def forward(side, origin, chunk):
            await_arrival(place(0, origin, chunk), pass_recvs.at[origin, chunk])
            passing(side, origin, chunk).start()

        def moment(now, carry):
            for distance in range(1, heads - 1):
                for side in range(2):
                    each_passing(side, distance, now - distance, forward)

            @pl.when(now < passed_on)
            def _():
                await_arrival(place(0, me, now), own_recvs.at[0, now])

            @pl.when((now >= passed_on) & (now < chunks))
            def _():
                relay(0, now)

            for side in range(2):
                each_passing(side, 0, now, lambda *which: passing(*which).start())
            return carry

        lax.fori_loop(0, chunks + heads - 2, moment, 0)

    def settle_first_block():
        def settle_passing(side, origin, chunk):
            await_sent(as_many(1, passed_on), pass_sends.at[side, origin])

        for distance in range(heads - 1):
            for side in range(2):
                each_passing(side, distance, 0, settle_passing)

    def relay(span, chunk):
        await_arrival(place(span, me, chunk), own_recvs.at[span, chunk])

        @pl.when(jnp.logical_not(goes_straight(span, chunk)))
        def _():
            for step in range(1, heads):
                relay_copy(span, step, chunk).start()

    def project_keys(span):
        sums[0] = jnp.zeros(sums.shape[1:], jnp.float32)
        sums[1] = jnp.zeros(sums.shape[1:], jnp.float32)

        def block(step, squares):
            origin = lax.rem(me + step, heads)

            first = (segment > 0) & (span == 0)
            passed = jnp.where(origin < me, me + 1 < heads, me >= 1)

            @pl.when((step > 0) & jnp.logical_not(first))
            def _():
                await_arrival(whole.at[span, :, columns_of(origin)], arrivals.at[span, origin])

            @pl.when((step > 0) & first)
            def _():
                direct = pl.ds(passed_on * piece, (chunks - passed_on) * piece)
                await_arrival(
                    whole.at[span, direct, columns_of(origin)], arrivals.at[span, origin]
                )

            @pl.when((step > 0) & first & jnp.logical_not(passed))
            def _():
                def wait(chunk, carry):
                    await_arrival(place(span, origin, chunk), pass_recvs.at[origin, chunk])
                    return carry

                lax.fori_loop(0, passed_on, wait, 0)

            here = columns_of(origin)
            values = whole[span, :, here].astype(jnp.float32)
            scaled[:, here] = (values * in_gain_ref[:, here]).astype(jnp.bfloat16)
            sums[0] += dot(scaled[:, here], qkv[1, here, :])
            sums[1] += dot(scaled[:, here], qkv[2, here, :])
            return squares + jnp.sum(values * values, axis=1, keepdims=True)

        squares = lax.fori_loop(0, heads, block, jnp.zeros((rows, 1), jnp.float32))
        row_scale[...] = lax.rsqrt(squares * (1.0 / features) + norm_eps)

    def rows_at(origin, count=1):
        return pl.ds(pl.multiple_of(origin * rows, rows), count * rows)

    def far_copy(span, part, step):
        return remote(
            both.at[span, part, rows_at(place_seq), :],
            both.at[span, part, rows_at(place_seq), :],
            far_sends.at[span],
            far_recvs.at[span, part, step],
            {"seq": 2 * lax.rem(chip + step, chips) + core},
        )

    def near_copy(span, part, step):
        origin = 2 * lax.rem(chip + chips - step, chips) + core
        return remote(
            both.at[span, part, rows_at(origin), :],
            both.at[span, part, rows_at(origin), :],
            near_sends.at[span],
            near_recvs.at[span, step],
            partner,
        )

    def project_pair(span):
        project_keys(span)
        scale = row_scale[...]
        own = rows_at(place_seq)
        both[span, 0, own, :] = (rms_scale(sums[0] * scale) * qk_gain_ref[1:2, :]).astype(jnp.bfloat16)
        diagonal = lax.broadcasted_iota(jnp.int32, (rows, rows), 0) == lax.broadcasted_iota(
            jnp.int32, (rows, rows), 1
        )
        rates = jnp.sum(
            jnp.where(diagonal, rate_ref[pl.ds(span, 1), :], 0.0), axis=1, keepdims=True
        )
        both[span, 1, own, :] = (-rates * (sums[1] * scale)).astype(jnp.bfloat16)
        for part in range(2):
            for step in range(1, chips):
                far_copy(span, part, step).start()
        for part in range(2):
            near_copy(span, part, 0).start()

    def project_queries():
        queries[...] = (rms_scale(dot(scaled[...], qkv[0]) * row_scale[...]) * qk_gain_ref[0:1, :]).astype(jnp.bfloat16)

    def finish(span, chunk):
        here = rows_of(chunk)
        total = whole[span, here, columns_of(me)].astype(jnp.float32) + terms[
            span, me, here, :
        ].astype(jnp.float32)
        await_arrival(as_many(heads - 1, 1), term_recvs.at[span, chunk])
        for step in range(1, heads):
            origin = other_head(step)
            total += slots[span, origin, here, :].astype(jnp.float32)
        result_ref[span, here, :] = total.astype(jnp.bfloat16)

        @pl.when(segment < last_segment)
        def _():
            hop(span, 0, chunk).start()

            @pl.when(goes_straight(span, chunk))
            def _():
                for step in range(1, heads):
                    hop(span, step, chunk).start()

    def term_copy(span, step, chunk):
        target = other_head(step)
        return remote(
            terms.at[span, target, rows_of(chunk), :],
            slots.at[span, me, rows_of(chunk), :],
            term_sends.at[span],
            term_recvs.at[span, chunk],
            {"head": target},
        )

    def hop(span, step, chunk):
        return remote(
            result_ref.at[span, rows_of(chunk), :],
            place(span, me, chunk),
            straight_sends.at[span] if step else hop_sends.at[span],
            arrivals.at[span, me] if step else own_recvs.at[span, chunk],
            {"segment": segment + 1, "head": other_head(step) if step else me},
        )

    def finish_some(span, first, count):
        @pl.when((segment < last_segment) & (span > 0))
        def _():
            def one(index, carry):
                finish(span - 1, first + index)
                return carry

            lax.fori_loop(0, count, one, 0)

    def relay_some(span, first, count):
        @pl.when((segment > 0) & (span + 1 < spans))
        def _():
            def one(index, carry):
                relay(span + 1, first + index)
                return carry

            lax.fori_loop(0, count, one, 0)

    def gradients(span, step):
        for part in range(2):

            @pl.when(step > 0)
            def _():
                there = rows_at(2 * lax.rem(chip + chips - step, chips) + core)
                await_arrival(both.at[span, part, there, :], far_recvs.at[span, part, step])
                near_copy(span, part, step).start()

        origin = lax.rem(chip + chips - step, chips)
        await_arrival(
            both.at[span, :, rows_at(2 * origin + 1 - core), :], near_recvs.at[span, step]
        )
        here = rows_at(2 * origin, 2)
        keys = both[span, 0, here, :]
        grads = both[span, 1, here, :]
        pre_gate = dot(keys, work[0])
        pre_up = dot(keys, work[1])
        backward = dot(grads, work[2])
        sigmoid_gate = jax.nn.sigmoid(pre_gate)
        gated = pre_gate * sigmoid_gate
        rights[0, here, :] = (
            backward * pre_up * sigmoid_gate * (1.0 + pre_gate * (1.0 - sigmoid_gate))
        ).astype(jnp.bfloat16)
        rights[1, here, :] = (backward * gated).astype(jnp.bfloat16)
        rights[2, here, :] = (gated * pre_up).astype(jnp.bfloat16)

    def symmetric(upper, last_block):
        return jnp.concatenate(
            [upper, jnp.concatenate([upper[:, half:].T, last_block], axis=1)], axis=0
        )

    def mixed(gram, square):
        return (ns_second * gram.astype(jnp.float32) + ns_third * square).astype(jnp.bfloat16)

    half = work.shape[1] // 2

    def orthogonalize(span):
        raw = [contract(both[span, index // 2], rights[index], (0, 0)) for index in range(3)]
        scales = [
            1.0 / (jnp.sqrt(jnp.sum(gradient * gradient, keepdims=True)) + grad_eps)
            for gradient in raw
        ]
        for index in range(3):
            work[index] = (raw[index] * scales[index]).astype(jnp.bfloat16)

        def sweep(step, inner):
            finish_some(span, (4 + step) * unit, unit)
            relay_some(span, (3 + step) * unit, (1 + step) * unit)
            current = [work[index] for index in range(3)]
            grams = [
                symmetric(
                    contract(matrix[:half], matrix, (1, 1)).astype(jnp.bfloat16),
                    contract(matrix[half:], matrix[half:], (1, 1)).astype(jnp.bfloat16),
                )
                for matrix in current
            ]
            mixings = [
                symmetric(mixed(gram[:half], dot(gram[:half], gram)), mixed(gram[half:, half:], dot(gram[half:], gram[:, half:])))
                for gram in grams
            ]
            for index in range(3):
                work[index] = (
                    ns_first * current[index].astype(jnp.float32)
                    + dot(mixings[index], current[index])
                ).astype(jnp.bfloat16)
            return inner

        lax.fori_loop(0, NS_STEPS, sweep, 0)

    def update():
        inner, wide = work.shape[1:]

        def moved(index, here, there):
            return state[index, here, there] - update_step * work[index, here, there].astype(
                jnp.float32
            )

        def store(index, here, there, fresh):
            work[index, here, there] = fresh.astype(jnp.bfloat16)
            state[index, here, there] = fresh

        for index in range(2):
            for column in range(0, wide, 256):
                there = slice(column, column + 256)
                squares = jnp.zeros((1, 256), jnp.float32)
                for row in range(0, inner, 64):
                    part = moved(index, slice(row, row + 64), there)
                    squares += jnp.sum(part * part, axis=0, keepdims=True)
                factor = wide_norms[index, :, there] / (jnp.sqrt(squares) + norm_eps)
                for row in range(0, inner, 64):
                    here = slice(row, row + 64)
                    store(index, here, there, moved(index, here, there) * factor)
        for row in range(0, inner, 32):
            here = slice(row, row + 32)
            part = moved(2, here, slice(None))
            length = jnp.sqrt(jnp.sum(part * part, axis=1, keepdims=True)) + norm_eps
            store(2, here, slice(None), part * (down_norm[here, :] / length))

    def read_out(span):
        gate_out = dot(queries[...], work[0])
        up_out = dot(queries[...], work[1])
        inner = (gate_out * jax.nn.sigmoid(gate_out) * up_out).astype(jnp.bfloat16)
        output = contract(inner, work[2], (1, 1))
        normed_out = (rms_scale(output) * out_gain_ref[...]).astype(jnp.bfloat16)

        for origin in range(heads):
            terms[span, origin] = dot(
                normed_out, out_weights[:, origin * width : (origin + 1) * width]
            ).astype(jnp.bfloat16)
    def detours(span, chunk):
        return (segment == last_segment) & (chunk >= chunks - around)

    def steps_aside(span, chunk):
        if segments == 1:
            return segment < 0
        return (segment == 0) & (span == 0) & ((chunk // unit == 2) | (chunk // unit == 4))

    def aside_chunk(place_at):
        return (2 + 2 * (place_at // unit)) * unit + lax.rem(place_at, unit)

    def aside_rows(place_at):
        return pl.ds(pl.multiple_of(place_at * piece, piece), piece)

    def aside_copy(step, place_at):
        return remote(
            terms.at[0, other_head(step), rows_of(aside_chunk(place_at)), :],
            aside.at[step, aside_rows(place_at), :],
            aside_sends.at[0],
            aside_recvs.at[place_at],
            {"segment": 1},
        )

    def aside_onward(step, place_at):
        return remote(
            aside.at[step, aside_rows(place_at), :],
            slots.at[0, me, rows_of(aside_chunk(place_at)), :],
            aside_sends.at[0],
            term_recvs.at[0, aside_chunk(place_at)],
            {"segment": 0, "head": other_head(step)},
        )

    def each_aside(action):
        def one(place_at, carry):
            for step in range(1, heads):
                action(step, place_at).start()
            return carry

        lax.fori_loop(0, 2 * unit, one, 0)

    def pass_aside():
        def one(place_at, carry):
            await_arrival(as_many(heads - 1, 1), aside_recvs.at[place_at])
            for step in range(1, heads):
                aside_onward(step, place_at).start()
            return carry

        lax.fori_loop(0, 2 * unit, one, 0)

    def settle_aside():
        await_sent(as_many(heads - 1, 2 * unit), aside_sends.at[0])

    def around_rows(chunk):
        return pl.ds(pl.multiple_of((chunk - (chunks - around)) * piece, piece), piece)

    def around_copy(span, step, chunk):
        return remote(
            terms.at[span, other_head(step), rows_of(chunk), :],
            via.at[span, step, around_rows(chunk), :],
            around_sends.at[span],
            around_recvs.at[span, chunk - (chunks - around)],
            {"segment": last_segment - 1},
        )

    def around_onward(span, step, chunk):
        return remote(
            via.at[span, step, around_rows(chunk), :],
            slots.at[span, me, rows_of(chunk), :],
            around_sends.at[span],
            term_recvs.at[span, chunk],
            {"segment": last_segment, "head": other_head(step)},
        )

    def send_terms(span):
        def send(index, carry):
            chunk = chunks - 1 - index

            @pl.when(detours(span, chunk))
            def _():
                for step in range(1, heads):
                    around_copy(span, step, chunk).start()

            return carry

        if around:
            lax.fori_loop(0, around, send, 0)

            @pl.when((segment == 0) & (span == 0))
            def _():
                each_aside(aside_copy)

        def send_straight(chunk, carry):
            @pl.when(jnp.logical_not(detours(span, chunk) | steps_aside(span, chunk)))
            def _():
                for step in range(1, heads):
                    term_copy(span, step, chunk).start()

            return carry

        lax.fori_loop(0, chunks, send_straight, 0)

    @pl.when(segment == 0)
    def _():
        for span in range(spans):
            own_copy(span).wait()

    @pl.when(segment > 0)
    def _():
        settle_spread(0)
        for span in range(1, spans):
            pl.semaphore_wait(ready, heads - 1)
            start_spread(span)
            settle_spread(span)

        @pl.when(segment == 1)
        def _():
            pass_aside()

        pass_first_block()

    for part in (1, 2, 0):
        loads[part].wait()
    out_load.wait()

    def block(span, carry):
        @pl.when((segment > 0) | (span == 0))
        def _():
            project_pair(span)

        @pl.when((segment == last_segment) & (span > 0))
        def _():
            send_terms(span - 1)

        @pl.when((segment == 0) & (span + 1 < spans))
        def _():
            start_spread(span + 1)

            for away in range(1, segments):
                for step in range(1, heads):
                    signal(ready, {"segment": away, "head": other_head(step)})

        relay_some(span, 0, unit)
        project_queries()

        def gradient_step(step, inner):
            gradients(span, step)

            @pl.when(step == 0)
            def _():
                finish_some(span, 0, 2 * unit)
                relay_some(span, unit, unit)

            return inner

        lax.fori_loop(0, chips, gradient_step, 0)
        finish_some(span, 2 * unit, 2 * unit)
        relay_some(span, 2 * unit, unit)
        orthogonalize(span)
        finish_some(span, 6 * unit, 2 * unit)

        update()
        read_out(span)
        relay_some(span, 6 * unit, 2 * unit)

        @pl.when((segment < last_segment) | (span == spans - 1))
        def _():
            send_terms(span)

        @pl.when((segment == 0) & (span + 1 < spans))
        def _():
            project_pair(span + 1)

        return carry

    lax.fori_loop(0, spans, block, 0)

    @pl.when(segment == 0)
    def _():
        for span in range(spans):
            settle_spread(span)
        if segments > 1:
            settle_aside()

    @pl.when(segment > 0)
    def _():
        settle_first_block()
        await_sent(as_many(heads - 1, chunks - unit - passed_on), relay_sends.at[0])
        for span in range(1, spans):
            await_sent(as_many(heads - 1, chunks - 2 * unit), relay_sends.at[span])

        @pl.when(segment == 1)
        def _():
            settle_aside()

    def settle_terms(span):
        beside = 2 * unit if segments > 1 and span == 0 else 0

        @pl.when((segment > 0) & (segment < last_segment))
        def _():
            await_sent(as_many(heads - 1, chunks), term_sends.at[span])

        @pl.when((segment == 0) & (segment < last_segment))
        def _():
            await_sent(as_many(heads - 1, chunks - beside), term_sends.at[span])

        @pl.when(segment == last_segment)
        def _():
            await_sent(as_many(heads - 1, chunks - around), term_sends.at[span])
            if around:
                await_sent(as_many(heads - 1, around), around_sends.at[span])

    def settle_hops(span):
        @pl.when(segment < last_segment)
        def _():
            await_sent(as_many(1, chunks), hop_sends.at[span])
            await_sent(as_many(heads - 1, 2 * unit if span else unit), straight_sends.at[span])

    for span in range(spans):
        if span + 1 < spans:
            settle_terms(span)
            settle_hops(span)
        if chips > 1:
            await_sent(both.at[span, :, pl.ds(0, (chips - 1) * rows), :], far_sends.at[span])
        await_sent(both.at[span, :, pl.ds(0, chips * rows), :], near_sends.at[span])

    def last(index, carry):
        finish(index // chunks, lax.rem(index, chunks))
        return carry

    lax.fori_loop(jnp.where(segment < last_segment, (spans - 1) * chunks, 0), spans * chunks, last, 0)

    if around:

        @pl.when(segment == last_segment - 1)
        def _():
            def pass_on(index, carry):
                span, chunk = index // around, chunks - 1 - lax.rem(index, around)
                await_arrival(
                    as_many(heads - 1, 1), around_recvs.at[span, chunk - (chunks - around)]
                )
                for step in range(1, heads):
                    around_onward(span, step, chunk).start()
                return carry

            lax.fori_loop(0, spans * around, pass_on, 0)
            for span in range(spans):
                await_sent(as_many(heads - 1, around), around_sends.at[span])

    settle_terms(spans - 1)
    settle_hops(spans - 1)


def shards(stream, in_gain, w_qkv, qk_gain, w_one, w_three, w_two, token_rate, out_gain, w_out):
    segments = lax.axis_size("segment")
    devices = lax.axis_size("seq")
    heads = lax.axis_size("head")
    spans, rows, width = stream.shape
    features = w_qkv.shape[1]
    inner, wide = w_one.shape[2:]
    tokens = devices * rows
    chunks = 8
    vmem = pl.BlockSpec(memory_space=pltpu.VMEM)
    anywhere = pl.BlockSpec(memory_space=pl.ANY)
    low = jnp.bfloat16
    dma = pltpu.SemaphoreType.DMA
    result = pl.pallas_call(
        functools.partial(step_kernel, segments, devices, heads, chunks),
        name="step",
        out_shape=jax.ShapeDtypeStruct(stream.shape, low),
        in_specs=[anywhere, vmem, anywhere, vmem, anywhere, anywhere, anywhere, vmem, vmem, anywhere],
        out_specs=vmem,
        scratch_shapes=[
            pltpu.VMEM((3, features, inner), low),
            pltpu.VMEM((inner, features), low),
            pltpu.VMEM((2, inner, wide), low),
            pltpu.VMEM((wide, inner), low),
            pltpu.VMEM((spans, rows, features), low),
            pltpu.VMEM((rows, features), low),
            pltpu.VMEM((rows, 1), jnp.float32),
            pltpu.VMEM((2, rows, inner), jnp.float32),
            pltpu.VMEM((spans, 2, tokens, inner), low),
            pltpu.VMEM((rows, inner), low),
            pltpu.VMEM((3, tokens, wide), low),
            pltpu.VMEM((3, inner, wide), low),
            pltpu.VMEM((3, inner, wide), jnp.float32),
            pltpu.VMEM((2, 1, wide), jnp.float32),
            pltpu.VMEM((inner, 1), jnp.float32),
            pltpu.VMEM((spans, heads, rows, width), low),
            pltpu.VMEM((spans, heads, rows, width), low),
            dma((3,)),
            dma((4,)),
            dma((spans,)),
            dma((spans,)),
            dma((spans, heads)),
            dma((spans, chunks)),
            dma((heads, chunks)),
            dma((spans,)),
            dma((spans, 2, devices // 2)),
            dma((spans,)),
            dma((spans, devices // 2)),
            dma((spans,)),
            dma((spans, chunks)),
            dma((spans,)),
            dma((spans,)),
            dma((spans,)),
            dma((spans,)),
            dma((spans, 3 * (chunks // 8))),
            pltpu.SemaphoreType.REGULAR,
            dma((2, heads)),
            dma((1,)),
            dma((chunks // 4,)),
            pltpu.VMEM((heads, rows // 4, width), low),
        ]
        + ([pltpu.VMEM((spans, heads, 3 * (chunks // 8) * (rows // chunks), width), low)] if segments > 1 else []),
        compiler_params=pltpu.CompilerParams(
            collective_id=0, has_side_effects=True, vmem_limit_bytes=67043328
        ),
    )(
        stream,
        in_gain,
        jnp.transpose(w_qkv[0, :, 0], (1, 0, 2)),
        qk_gain[0, 0],
        w_one[0, 0],
        w_three[0, 0],
        w_two[0, 0],
        token_rate[0],
        out_gain[0, :1],
        w_out[0, 0],
    )
    return result[None]


def solution(mesh):
    placed = (
        P(None, "seq", "head"),
        P("segment", None),
        P("segment", None, "head", None, None),
        P("segment", "head", None, None),
        P("segment", "head", None, None),
        P("segment", "head", None, None),
        P("segment", "head", None, None),
        P("segment", None, "seq"),
        P("segment", "head", None),
        P("segment", "head", None, None),
    )
    return jax.shard_map(
        shards,
        mesh=mesh,
        in_specs=placed,
        out_specs=P("segment", None, "seq", "head"),
        check_vma=False,
    )
```

```python
import functools

import jax
import jax.numpy as jnp
from jax import lax
from jax.experimental import pallas as pl
from jax.experimental.pallas import tpu as pltpu
from jax.sharding import PartitionSpec as P

NS_STEPS = 2

ns_first = 3.4445
ns_second = -4.775
ns_third = 2.0315
update_step = 1.0
norm_eps = 1e-06
grad_eps = 1e-07


def rms_scale(values):
    return values * lax.rsqrt(jnp.mean(values * values, axis=-1, keepdims=True) + norm_eps)


def dot(left, right):
    return jnp.dot(left, right, preferred_element_type=jnp.float32)


def contract(left, right, dims):
    return lax.dot_general(
        left, right, ((dims[:1], dims[1:]), ((), ())), preferred_element_type=jnp.float32
    )


def signal(semaphore, target):
    pl.semaphore_signal(
        semaphore, inc=1, device_id=target, device_id_type=pl.DeviceIdType.MESH
    )


def remote(source, target, send_sem, recv_sem, device):
    return pltpu.make_async_remote_copy(
        src_ref=source,
        dst_ref=target,
        send_sem=send_sem,
        recv_sem=recv_sem,
        device_id=device,
        device_id_type=pl.DeviceIdType.MESH,
    )


def step_kernel(
    segments,
    devices,
    heads,
    chunks,
    stream_hbm,
    in_gain_ref,
    qkv_hbm,
    qk_gain_ref,
    gate_hbm,
    up_hbm,
    down_hbm,
    rate_ref,
    out_gain_ref,
    out_hbm,
    result_ref,
    qkv,
    out_weights,
    wide_init,
    down_init,
    whole,
    scaled,
    row_scale,
    sums,
    both,
    queries,
    rights,
    work,
    state,
    wide_norms,
    down_norm,
    terms,
    slots,
    qkv_sems,
    load_sems,
    own_sems,
    spread_sends,
    arrivals,
    own_recvs,
    pass_recvs,
    far_sends,
    far_recvs,
    near_sends,
    near_recvs,
    term_sends,
    term_recvs,
    hop_sends,
    straight_sends,
    relay_sends,
    around_sends,
    around_recvs,
    ready,
    pass_sends,
    aside_sends,
    aside_recvs,
    aside,
    *vias,
):
    segment = lax.axis_index("segment")
    place_seq = lax.axis_index("seq")
    me = lax.axis_index("head")
    spans, rows, width = result_ref.shape
    features = whole.shape[2]
    chips = devices // 2
    chip, core = place_seq // 2, lax.rem(place_seq, 2)
    partner = {"seq": 2 * chip + 1 - core}
    piece = rows // chunks
    unit = chunks // 8
    around = 3 * unit if segments > 1 else 0
    via = vias[0] if around else None
    last_segment = segments - 1

    loads = [pltpu.make_async_copy(qkv_hbm.at[part], qkv.at[part], qkv_sems.at[part]) for part in range(3)]
    fast_loads = [
        pltpu.make_async_copy(gate_hbm, wide_init.at[0], load_sems.at[0]),
        pltpu.make_async_copy(up_hbm, wide_init.at[1], load_sems.at[1]),
        pltpu.make_async_copy(down_hbm, down_init, load_sems.at[2]),
    ]
    out_load = pltpu.make_async_copy(out_hbm, out_weights, load_sems.at[3])
    for copy in fast_loads:
        copy.start()

    def other_head(step):
        up, down = step - 1, heads - step
        upward = jnp.where(up >= me, up + 1, up)
        downward = jnp.where(down > me, down, down - 1)
        return jnp.where(2 * me < heads, downward, upward)

    barrier = pltpu.get_barrier_semaphore()
    for away in range(segments):
        for step in range(heads):
            if away or step:
                signal(
                    barrier,
                    {"segment": lax.rem(segment + away, segments), "head": lax.rem(me + step, heads)},
                )
    for step in range(1, chips):
        signal(barrier, {"seq": 2 * lax.rem(chip + step, chips) + core})
    signal(barrier, partner)
    pl.semaphore_wait(barrier, segments * heads - 1 + chips)

    def columns_of(origin):
        return pl.ds(pl.multiple_of(origin * width, width), width)

    def rows_of(chunk):
        if isinstance(chunk, int):
            return pl.ds(chunk * piece, piece)
        return pl.ds(pl.multiple_of(chunk * piece, piece), piece)

    def place(span, origin, chunk):
        return whole.at[span, rows_of(chunk), columns_of(origin)]

    def await_arrival(like, semaphore):
        remote(like, like, semaphore, semaphore, partner).wait_recv()

    def await_sent(like, semaphore):
        remote(like, like, semaphore, semaphore, partner).wait_send()

    def as_many(blocks, count):
        return terms.at[0, pl.ds(0, blocks), pl.ds(0, count * piece), :]

    def spread(span, step, chunk):
        return remote(
            stream_hbm.at[span, rows_of(chunk), :],
            place(span, me, chunk),
            spread_sends.at[span],
            arrivals.at[span, me],
            {"segment": 0, "head": other_head(step)},
        )

    share = chunks // segments

    def start_spread(span):
        def one(index, carry):
            for step in range(1, heads):
                spread(span, step, segment * share + index).start()
            return carry

        lax.fori_loop(0, share, one, 0)

    def settle_spread(span):
        await_sent(as_many(heads - 1, share), spread_sends.at[span])

    start_spread(0)
    for part in (1, 2, 0):
        loads[part].start()
    out_load.start()

    def own_copy(span):
        return pltpu.make_async_copy(
            stream_hbm.at[span], whole.at[span, :, columns_of(me)], own_sems.at[span]
        )

    @pl.when(segment == 0)
    def _():
        for span in range(spans):
            own_copy(span).start()

    for copy in fast_loads:
        copy.wait()
    for index in range(2):
        work[index] = wide_init[index]
        wide = wide_init[index].astype(jnp.float32)
        state[index] = wide
        wide_norms[index] = jnp.sqrt(jnp.sum(wide * wide, axis=0, keepdims=True))
    down = down_init[...].T
    work[2] = down
    down = down.astype(jnp.float32)
    state[2] = down
    down_norm[...] = jnp.sqrt(jnp.sum(down * down, axis=1, keepdims=True))

    def goes_straight(span, chunk):
        return chunk >= chunks - jnp.where(span > 0, 2 * unit, unit)

    def relay_copy(span, step, chunk):
        return remote(
            place(span, me, chunk),
            place(span, me, chunk),
            relay_sends.at[span],
            arrivals.at[span, me],
            {"head": other_head(step)},
        )

    def passing(side, origin, chunk):
        return remote(
            place(0, origin, chunk),
            place(0, origin, chunk),
            pass_sends.at[side, origin],
            pass_recvs.at[origin, chunk],
            {"head": me + 1 - 2 * side},
        )

    has_next = (me + 1 < heads, me >= 1)
    passed_on = chunks - 5 * unit

    def each_passing(side, distance, chunk, action):
        origin = me - distance * (1 - 2 * side)

        @pl.when(
            (chunk >= 0) & (chunk < passed_on) & (origin >= 0) & (origin < heads) & has_next[side]
        )
        def _():
            action(side, origin, chunk)

    def pass_first_block():
        def forward(side, origin, chunk):
            await_arrival(place(0, origin, chunk), pass_recvs.at[origin, chunk])
            passing(side, origin, chunk).start()

        def moment(now, carry):
            for distance in range(1, heads - 1):
                for side in range(2):
                    each_passing(side, distance, now - distance, forward)

            @pl.when(now < passed_on)
            def _():
                await_arrival(place(0, me, now), own_recvs.at[0, now])

            @pl.when((now >= passed_on) & (now < chunks))
            def _():
                relay(0, now)

            for side in range(2):
                each_passing(side, 0, now, lambda *which: passing(*which).start())
            return carry

        lax.fori_loop(0, chunks + heads - 2, moment, 0)

    def settle_first_block():
        def settle_passing(side, origin, chunk):
            await_sent(as_many(1, passed_on), pass_sends.at[side, origin])

        for distance in range(heads - 1):
            for side in range(2):
                each_passing(side, distance, 0, settle_passing)

    def relay(span, chunk):
        await_arrival(place(span, me, chunk), own_recvs.at[span, chunk])

        @pl.when(jnp.logical_not(goes_straight(span, chunk)))
        def _():
            for step in range(1, heads):
                relay_copy(span, step, chunk).start()

    def project_keys(span):
        sums[0] = jnp.zeros(sums.shape[1:], jnp.float32)
        sums[1] = jnp.zeros(sums.shape[1:], jnp.float32)

        def block(step, squares):
            origin = lax.rem(me + step, heads)

            first = (segment > 0) & (span == 0)
            passed = jnp.where(origin < me, me + 1 < heads, me >= 1)

            @pl.when((step > 0) & jnp.logical_not(first))
            def _():
                await_arrival(whole.at[span, :, columns_of(origin)], arrivals.at[span, origin])

            @pl.when((step > 0) & first)
            def _():
                direct = pl.ds(passed_on * piece, (chunks - passed_on) * piece)
                await_arrival(
                    whole.at[span, direct, columns_of(origin)], arrivals.at[span, origin]
                )

            @pl.when((step > 0) & first & jnp.logical_not(passed))
            def _():
                def wait(chunk, carry):
                    await_arrival(place(span, origin, chunk), pass_recvs.at[origin, chunk])
                    return carry

                lax.fori_loop(0, passed_on, wait, 0)

            here = columns_of(origin)
            values = whole[span, :, here].astype(jnp.float32)
            scaled[:, here] = (values * in_gain_ref[:, here]).astype(jnp.bfloat16)
            sums[0] += dot(scaled[:, here], qkv[1, here, :])
            sums[1] += dot(scaled[:, here], qkv[2, here, :])
            return squares + jnp.sum(values * values, axis=1, keepdims=True)

        squares = lax.fori_loop(0, heads, block, jnp.zeros((rows, 1), jnp.float32))
        row_scale[...] = lax.rsqrt(squares * (1.0 / features) + norm_eps)

    def rows_at(origin, count=1):
        return pl.ds(pl.multiple_of(origin * rows, rows), count * rows)

    def far_copy(span, part, step):
        return remote(
            both.at[span, part, rows_at(place_seq), :],
            both.at[span, part, rows_at(place_seq), :],
            far_sends.at[span],
            far_recvs.at[span, part, step],
            {"seq": 2 * lax.rem(chip + step, chips) + core},
        )

    def near_copy(span, part, step):
        origin = 2 * lax.rem(chip + chips - step, chips) + core
        return remote(
            both.at[span, part, rows_at(origin), :],
            both.at[span, part, rows_at(origin), :],
            near_sends.at[span],
            near_recvs.at[span, step],
            partner,
        )

    def project_pair(span):
        project_keys(span)
        scale = row_scale[...]
        own = rows_at(place_seq)
        both[span, 0, own, :] = (rms_scale(sums[0] * scale) * qk_gain_ref[1:2, :]).astype(jnp.bfloat16)
        diagonal = lax.broadcasted_iota(jnp.int32, (rows, rows), 0) == lax.broadcasted_iota(
            jnp.int32, (rows, rows), 1
        )
        rates = jnp.sum(
            jnp.where(diagonal, rate_ref[pl.ds(span, 1), :], 0.0), axis=1, keepdims=True
        )
        both[span, 1, own, :] = (-rates * (sums[1] * scale)).astype(jnp.bfloat16)
        for part in range(2):
            for step in range(1, chips):
                far_copy(span, part, step).start()
        for part in range(2):
            near_copy(span, part, 0).start()

    def project_queries():
        queries[...] = (rms_scale(dot(scaled[...], qkv[0]) * row_scale[...]) * qk_gain_ref[0:1, :]).astype(jnp.bfloat16)

    def finish(span, chunk):
        here = rows_of(chunk)
        total = whole[span, here, columns_of(me)].astype(jnp.float32) + terms[
            span, me, here, :
        ].astype(jnp.float32)
        await_arrival(as_many(heads - 1, 1), term_recvs.at[span, chunk])
        for step in range(1, heads):
            origin = other_head(step)
            total += slots[span, origin, here, :].astype(jnp.float32)
        result_ref[span, here, :] = total.astype(jnp.bfloat16)

        @pl.when(segment < last_segment)
        def _():
            hop(span, 0, chunk).start()

            @pl.when(goes_straight(span, chunk))
            def _():
                for step in range(1, heads):
                    hop(span, step, chunk).start()

    def term_copy(span, step, chunk):
        target = other_head(step)
        return remote(
            terms.at[span, target, rows_of(chunk), :],
            slots.at[span, me, rows_of(chunk), :],
            term_sends.at[span],
            term_recvs.at[span, chunk],
            {"head": target},
        )

    def hop(span, step, chunk):
        return remote(
            result_ref.at[span, rows_of(chunk), :],
            place(span, me, chunk),
            straight_sends.at[span] if step else hop_sends.at[span],
            arrivals.at[span, me] if step else own_recvs.at[span, chunk],
            {"segment": segment + 1, "head": other_head(step) if step else me},
        )

    def finish_some(span, first, count):
        @pl.when((segment < last_segment) & (span > 0))
        def _():
            def one(index, carry):
                finish(span - 1, first + index)
                return carry

            lax.fori_loop(0, count, one, 0)

    def relay_some(span, first, count):
        @pl.when((segment > 0) & (span + 1 < spans))
        def _():
            def one(index, carry):
                relay(span + 1, first + index)
                return carry

            lax.fori_loop(0, count, one, 0)

    def gradients(span, step):
        for part in range(2):

            @pl.when(step > 0)
            def _():
                there = rows_at(2 * lax.rem(chip + chips - step, chips) + core)
                await_arrival(both.at[span, part, there, :], far_recvs.at[span, part, step])
                near_copy(span, part, step).start()

        origin = lax.rem(chip + chips - step, chips)
        await_arrival(
            both.at[span, :, rows_at(2 * origin + 1 - core), :], near_recvs.at[span, step]
        )
        here = rows_at(2 * origin, 2)
        keys = both[span, 0, here, :]
        grads = both[span, 1, here, :]
        pre_gate = dot(keys, work[0])
        pre_up = dot(keys, work[1])
        backward = dot(grads, work[2])
        sigmoid_gate = jax.nn.sigmoid(pre_gate)
        gated = pre_gate * sigmoid_gate
        rights[0, here, :] = (
            backward * pre_up * sigmoid_gate * (1.0 + pre_gate * (1.0 - sigmoid_gate))
        ).astype(jnp.bfloat16)
        rights[1, here, :] = (backward * gated).astype(jnp.bfloat16)
        rights[2, here, :] = (gated * pre_up).astype(jnp.bfloat16)

    def symmetric(upper, last_block):
        return jnp.concatenate(
            [upper, jnp.concatenate([upper[:, half:].T, last_block], axis=1)], axis=0
        )

    def mixed(gram, square):
        return (ns_second * gram.astype(jnp.float32) + ns_third * square).astype(jnp.bfloat16)

    half = work.shape[1] // 2

    def orthogonalize(span):
        raw = [contract(both[span, index // 2], rights[index], (0, 0)) for index in range(3)]
        scales = [
            1.0 / (jnp.sqrt(jnp.sum(gradient * gradient, keepdims=True)) + grad_eps)
            for gradient in raw
        ]
        for index in range(3):
            work[index] = (raw[index] * scales[index]).astype(jnp.bfloat16)

        def sweep(step, inner):
            finish_some(span, (3 + step) * unit, unit)
            relay_some(span, (3 + step) * unit, (1 + step) * unit)
            current = [work[index] for index in range(3)]
            grams = [
                symmetric(
                    contract(matrix[:half], matrix, (1, 1)).astype(jnp.bfloat16),
                    contract(matrix[half:], matrix[half:], (1, 1)).astype(jnp.bfloat16),
                )
                for matrix in current
            ]
            mixings = [
                symmetric(mixed(gram[:half], dot(gram[:half], gram)), mixed(gram[half:, half:], dot(gram[half:], gram[:, half:])))
                for gram in grams
            ]
            for index in range(3):
                work[index] = (
                    ns_first * current[index].astype(jnp.float32)
                    + dot(mixings[index], current[index])
                ).astype(jnp.bfloat16)
            return inner

        lax.fori_loop(0, NS_STEPS, sweep, 0)

    def update():
        inner, wide = work.shape[1:]

        def moved(index, here, there):
            return state[index, here, there] - update_step * work[index, here, there].astype(
                jnp.float32
            )

        def store(index, here, there, fresh):
            work[index, here, there] = fresh.astype(jnp.bfloat16)
            state[index, here, there] = fresh

        for index in range(2):
            for column in range(0, wide, 256):
                there = slice(column, column + 256)
                squares = jnp.zeros((1, 256), jnp.float32)
                for row in range(0, inner, 64):
                    part = moved(index, slice(row, row + 64), there)
                    squares += jnp.sum(part * part, axis=0, keepdims=True)
                factor = wide_norms[index, :, there] / (jnp.sqrt(squares) + norm_eps)
                for row in range(0, inner, 64):
                    here = slice(row, row + 64)
                    store(index, here, there, moved(index, here, there) * factor)
        for row in range(0, inner, 32):
            here = slice(row, row + 32)
            part = moved(2, here, slice(None))
            length = jnp.sqrt(jnp.sum(part * part, axis=1, keepdims=True)) + norm_eps
            store(2, here, slice(None), part * (down_norm[here, :] / length))

    def read_out(span):
        gate_out = dot(queries[...], work[0])
        up_out = dot(queries[...], work[1])
        inner = (gate_out * jax.nn.sigmoid(gate_out) * up_out).astype(jnp.bfloat16)
        output = contract(inner, work[2], (1, 1))
        normed_out = (rms_scale(output) * out_gain_ref[...]).astype(jnp.bfloat16)

        for origin in range(heads):
            terms[span, origin] = dot(
                normed_out, out_weights[:, origin * width : (origin + 1) * width]
            ).astype(jnp.bfloat16)
    def detours(span, chunk):
        return (segment == last_segment) & (chunk >= chunks - around)

    def steps_aside(span, chunk):
        if segments == 1:
            return segment < 0
        return (segment == 0) & (span == 0) & ((chunk // unit == 2) | (chunk // unit == 4))

    def aside_chunk(place_at):
        return (2 + 2 * (place_at // unit)) * unit + lax.rem(place_at, unit)

    def aside_rows(place_at):
        return pl.ds(pl.multiple_of(place_at * piece, piece), piece)

    def aside_copy(step, place_at):
        return remote(
            terms.at[0, other_head(step), rows_of(aside_chunk(place_at)), :],
            aside.at[step, aside_rows(place_at), :],
            aside_sends.at[0],
            aside_recvs.at[place_at],
            {"segment": 1},
        )

    def aside_onward(step, place_at):
        return remote(
            aside.at[step, aside_rows(place_at), :],
            slots.at[0, me, rows_of(aside_chunk(place_at)), :],
            aside_sends.at[0],
            term_recvs.at[0, aside_chunk(place_at)],
            {"segment": 0, "head": other_head(step)},
        )

    def each_aside(action):
        def one(place_at, carry):
            for step in range(1, heads):
                action(step, place_at).start()
            return carry

        lax.fori_loop(0, 2 * unit, one, 0)

    def pass_aside():
        def one(place_at, carry):
            await_arrival(as_many(heads - 1, 1), aside_recvs.at[place_at])
            for step in range(1, heads):
                aside_onward(step, place_at).start()
            return carry

        lax.fori_loop(0, 2 * unit, one, 0)

    def settle_aside():
        await_sent(as_many(heads - 1, 2 * unit), aside_sends.at[0])

    def around_rows(chunk):
        return pl.ds(pl.multiple_of((chunk - (chunks - around)) * piece, piece), piece)

    def around_copy(span, step, chunk):
        return remote(
            terms.at[span, other_head(step), rows_of(chunk), :],
            via.at[span, step, around_rows(chunk), :],
            around_sends.at[span],
            around_recvs.at[span, chunk - (chunks - around)],
            {"segment": last_segment - 1},
        )

    def around_onward(span, step, chunk):
        return remote(
            via.at[span, step, around_rows(chunk), :],
            slots.at[span, me, rows_of(chunk), :],
            around_sends.at[span],
            term_recvs.at[span, chunk],
            {"segment": last_segment, "head": other_head(step)},
        )

    def send_terms(span):
        def send(index, carry):
            chunk = chunks - 1 - index

            @pl.when(detours(span, chunk))
            def _():
                for step in range(1, heads):
                    around_copy(span, step, chunk).start()

            return carry

        if around:
            lax.fori_loop(0, around, send, 0)

            @pl.when((segment == 0) & (span == 0))
            def _():
                each_aside(aside_copy)

        def send_straight(chunk, carry):
            @pl.when(jnp.logical_not(detours(span, chunk) | steps_aside(span, chunk)))
            def _():
                for step in range(1, heads):
                    term_copy(span, step, chunk).start()

            return carry

        lax.fori_loop(0, chunks, send_straight, 0)

    @pl.when(segment == 0)
    def _():
        for span in range(spans):
            own_copy(span).wait()

    @pl.when(segment > 0)
    def _():
        settle_spread(0)
        for span in range(1, spans):
            pl.semaphore_wait(ready, heads - 1)
            start_spread(span)
            settle_spread(span)

        @pl.when(segment == 1)
        def _():
            pass_aside()

        pass_first_block()

    for part in (1, 2, 0):
        loads[part].wait()
    out_load.wait()

    def block(span, carry):
        @pl.when((segment > 0) | (span == 0))
        def _():
            project_pair(span)

        @pl.when((segment == last_segment) & (span > 0))
        def _():
            send_terms(span - 1)

        @pl.when((segment == 0) & (span + 1 < spans))
        def _():
            start_spread(span + 1)

            for away in range(1, segments):
                for step in range(1, heads):
                    signal(ready, {"segment": away, "head": other_head(step)})

        relay_some(span, 0, unit)
        project_queries()

        def gradient_step(step, inner):
            gradients(span, step)

            @pl.when(step == 0)
            def _():
                finish_some(span, 0, unit)
                relay_some(span, unit, unit)

            return inner

        lax.fori_loop(0, chips, gradient_step, 0)
        finish_some(span, unit, 2 * unit)
        relay_some(span, 2 * unit, unit)
        orthogonalize(span)
        finish_some(span, 5 * unit, 3 * unit)

        update()
        read_out(span)
        relay_some(span, 6 * unit, 2 * unit)

        @pl.when((segment < last_segment) | (span == spans - 1))
        def _():
            send_terms(span)

        @pl.when((segment == 0) & (span + 1 < spans))
        def _():
            project_pair(span + 1)

        return carry

    lax.fori_loop(0, spans, block, 0)

    @pl.when(segment == 0)
    def _():
        for span in range(spans):
            settle_spread(span)
        if segments > 1:
            settle_aside()

    @pl.when(segment > 0)
    def _():
        settle_first_block()
        await_sent(as_many(heads - 1, chunks - unit - passed_on), relay_sends.at[0])
        for span in range(1, spans):
            await_sent(as_many(heads - 1, chunks - 2 * unit), relay_sends.at[span])

        @pl.when(segment == 1)
        def _():
            settle_aside()

    def settle_terms(span):
        beside = 2 * unit if segments > 1 and span == 0 else 0

        @pl.when((segment > 0) & (segment < last_segment))
        def _():
            await_sent(as_many(heads - 1, chunks), term_sends.at[span])

        @pl.when((segment == 0) & (segment < last_segment))
        def _():
            await_sent(as_many(heads - 1, chunks - beside), term_sends.at[span])

        @pl.when(segment == last_segment)
        def _():
            await_sent(as_many(heads - 1, chunks - around), term_sends.at[span])
            if around:
                await_sent(as_many(heads - 1, around), around_sends.at[span])

    def settle_hops(span):
        @pl.when(segment < last_segment)
        def _():
            await_sent(as_many(1, chunks), hop_sends.at[span])
            await_sent(as_many(heads - 1, 2 * unit if span else unit), straight_sends.at[span])

    for span in range(spans):
        if span + 1 < spans:
            settle_terms(span)
            settle_hops(span)
        if chips > 1:
            await_sent(both.at[span, :, pl.ds(0, (chips - 1) * rows), :], far_sends.at[span])
        await_sent(both.at[span, :, pl.ds(0, chips * rows), :], near_sends.at[span])

    def last(index, carry):
        finish(index // chunks, lax.rem(index, chunks))
        return carry

    lax.fori_loop(jnp.where(segment < last_segment, (spans - 1) * chunks, 0), spans * chunks, last, 0)

    if around:

        @pl.when(segment == last_segment - 1)
        def _():
            def pass_on(index, carry):
                span, chunk = index // around, chunks - 1 - lax.rem(index, around)
                await_arrival(
                    as_many(heads - 1, 1), around_recvs.at[span, chunk - (chunks - around)]
                )
                for step in range(1, heads):
                    around_onward(span, step, chunk).start()
                return carry

            lax.fori_loop(0, spans * around, pass_on, 0)
            for span in range(spans):
                await_sent(as_many(heads - 1, around), around_sends.at[span])

    settle_terms(spans - 1)
    settle_hops(spans - 1)


def shards(stream, in_gain, w_qkv, qk_gain, w_one, w_three, w_two, token_rate, out_gain, w_out):
    segments = lax.axis_size("segment")
    devices = lax.axis_size("seq")
    heads = lax.axis_size("head")
    spans, rows, width = stream.shape
    features = w_qkv.shape[1]
    inner, wide = w_one.shape[2:]
    tokens = devices * rows
    chunks = 8
    vmem = pl.BlockSpec(memory_space=pltpu.VMEM)
    anywhere = pl.BlockSpec(memory_space=pl.ANY)
    low = jnp.bfloat16
    dma = pltpu.SemaphoreType.DMA
    result = pl.pallas_call(
        functools.partial(step_kernel, segments, devices, heads, chunks),
        name="step",
        out_shape=jax.ShapeDtypeStruct(stream.shape, low),
        in_specs=[anywhere, vmem, anywhere, vmem, anywhere, anywhere, anywhere, vmem, vmem, anywhere],
        out_specs=vmem,
        scratch_shapes=[
            pltpu.VMEM((3, features, inner), low),
            pltpu.VMEM((inner, features), low),
            pltpu.VMEM((2, inner, wide), low),
            pltpu.VMEM((wide, inner), low),
            pltpu.VMEM((spans, rows, features), low),
            pltpu.VMEM((rows, features), low),
            pltpu.VMEM((rows, 1), jnp.float32),
            pltpu.VMEM((2, rows, inner), jnp.float32),
            pltpu.VMEM((spans, 2, tokens, inner), low),
            pltpu.VMEM((rows, inner), low),
            pltpu.VMEM((3, tokens, wide), low),
            pltpu.VMEM((3, inner, wide), low),
            pltpu.VMEM((3, inner, wide), jnp.float32),
            pltpu.VMEM((2, 1, wide), jnp.float32),
            pltpu.VMEM((inner, 1), jnp.float32),
            pltpu.VMEM((spans, heads, rows, width), low),
            pltpu.VMEM((spans, heads, rows, width), low),
            dma((3,)),
            dma((4,)),
            dma((spans,)),
            dma((spans,)),
            dma((spans, heads)),
            dma((spans, chunks)),
            dma((heads, chunks)),
            dma((spans,)),
            dma((spans, 2, devices // 2)),
            dma((spans,)),
            dma((spans, devices // 2)),
            dma((spans,)),
            dma((spans, chunks)),
            dma((spans,)),
            dma((spans,)),
            dma((spans,)),
            dma((spans,)),
            dma((spans, 3 * (chunks // 8))),
            pltpu.SemaphoreType.REGULAR,
            dma((2, heads)),
            dma((1,)),
            dma((chunks // 4,)),
            pltpu.VMEM((heads, rows // 4, width), low),
        ]
        + ([pltpu.VMEM((spans, heads, 3 * (chunks // 8) * (rows // chunks), width), low)] if segments > 1 else []),
        compiler_params=pltpu.CompilerParams(
            collective_id=0, has_side_effects=True, vmem_limit_bytes=67043328
        ),
    )(
        stream,
        in_gain,
        jnp.transpose(w_qkv[0, :, 0], (1, 0, 2)),
        qk_gain[0, 0],
        w_one[0, 0],
        w_three[0, 0],
        w_two[0, 0],
        token_rate[0],
        out_gain[0, :1],
        w_out[0, 0],
    )
    return result[None]


def solution(mesh):
    placed = (
        P(None, "seq", "head"),
        P("segment", None),
        P("segment", None, "head", None, None),
        P("segment", "head", None, None),
        P("segment", "head", None, None),
        P("segment", "head", None, None),
        P("segment", "head", None, None),
        P("segment", None, "seq"),
        P("segment", "head", None),
        P("segment", "head", None, None),
    )
    return jax.shard_map(
        shards,
        mesh=mesh,
        in_specs=placed,
        out_specs=P("segment", None, "seq", "head"),
        check_vma=False,
    )
```

```python
import functools

import jax
import jax.numpy as jnp
from jax import lax
from jax.experimental import pallas as pl
from jax.experimental.pallas import tpu as pltpu
from jax.sharding import PartitionSpec as P

NS_STEPS = 2

ns_first = 3.4445
ns_second = -4.775
ns_third = 2.0315
update_step = 1.0
norm_eps = 1e-06
grad_eps = 1e-07


def rms_scale(values):
    return values * lax.rsqrt(jnp.mean(values * values, axis=-1, keepdims=True) + norm_eps)


def dot(left, right):
    return jnp.dot(left, right, preferred_element_type=jnp.float32)


def contract(left, right, dims):
    return lax.dot_general(
        left, right, ((dims[:1], dims[1:]), ((), ())), preferred_element_type=jnp.float32
    )


def signal(semaphore, target):
    pl.semaphore_signal(
        semaphore, inc=1, device_id=target, device_id_type=pl.DeviceIdType.MESH
    )


def remote(source, target, send_sem, recv_sem, device):
    return pltpu.make_async_remote_copy(
        src_ref=source,
        dst_ref=target,
        send_sem=send_sem,
        recv_sem=recv_sem,
        device_id=device,
        device_id_type=pl.DeviceIdType.MESH,
    )


def step_kernel(
    segments,
    devices,
    heads,
    chunks,
    stream_hbm,
    in_gain_ref,
    qkv_hbm,
    qk_gain_ref,
    gate_hbm,
    up_hbm,
    down_hbm,
    rate_ref,
    out_gain_ref,
    out_hbm,
    result_ref,
    qkv,
    out_weights,
    wide_init,
    down_init,
    whole,
    scaled,
    row_scale,
    sums,
    both,
    queries,
    rights,
    work,
    state,
    wide_norms,
    down_norm,
    terms,
    slots,
    qkv_sems,
    load_sems,
    own_sems,
    spread_sends,
    arrivals,
    own_recvs,
    pass_recvs,
    far_sends,
    far_recvs,
    near_sends,
    near_recvs,
    term_sends,
    term_recvs,
    hop_sends,
    straight_sends,
    relay_sends,
    around_sends,
    around_recvs,
    ready,
    pass_sends,
    aside_sends,
    aside_recvs,
    aside,
    *vias,
):
    segment = lax.axis_index("segment")
    place_seq = lax.axis_index("seq")
    me = lax.axis_index("head")
    spans, rows, width = result_ref.shape
    features = whole.shape[2]
    chips = devices // 2
    chip, core = place_seq // 2, lax.rem(place_seq, 2)
    partner = {"seq": 2 * chip + 1 - core}
    piece = rows // chunks
    unit = chunks // 8
    around = 3 * unit if segments > 1 else 0
    via = vias[0] if around else None
    last_segment = segments - 1

    loads = [pltpu.make_async_copy(qkv_hbm.at[part], qkv.at[part], qkv_sems.at[part]) for part in range(3)]
    fast_loads = [
        pltpu.make_async_copy(gate_hbm, wide_init.at[0], load_sems.at[0]),
        pltpu.make_async_copy(up_hbm, wide_init.at[1], load_sems.at[1]),
        pltpu.make_async_copy(down_hbm, down_init, load_sems.at[2]),
    ]
    out_load = pltpu.make_async_copy(out_hbm, out_weights, load_sems.at[3])
    for copy in fast_loads:
        copy.start()

    def other_head(step):
        up, down = step - 1, heads - step
        upward = jnp.where(up >= me, up + 1, up)
        downward = jnp.where(down > me, down, down - 1)
        return jnp.where(2 * me < heads, downward, upward)

    barrier = pltpu.get_barrier_semaphore()
    for away in range(segments):
        for step in range(heads):
            if away or step:
                signal(
                    barrier,
                    {"segment": lax.rem(segment + away, segments), "head": lax.rem(me + step, heads)},
                )
    for step in range(1, chips):
        signal(barrier, {"seq": 2 * lax.rem(chip + step, chips) + core})
    signal(barrier, partner)
    pl.semaphore_wait(barrier, segments * heads - 1 + chips)

    def columns_of(origin):
        return pl.ds(pl.multiple_of(origin * width, width), width)

    def rows_of(chunk):
        if isinstance(chunk, int):
            return pl.ds(chunk * piece, piece)
        return pl.ds(pl.multiple_of(chunk * piece, piece), piece)

    def place(span, origin, chunk):
        return whole.at[span, rows_of(chunk), columns_of(origin)]

    def await_arrival(like, semaphore):
        remote(like, like, semaphore, semaphore, partner).wait_recv()

    def await_sent(like, semaphore):
        remote(like, like, semaphore, semaphore, partner).wait_send()

    def as_many(blocks, count):
        return terms.at[0, pl.ds(0, blocks), pl.ds(0, count * piece), :]

    def spread(span, step, chunk):
        return remote(
            stream_hbm.at[span, rows_of(chunk), :],
            place(span, me, chunk),
            spread_sends.at[span],
            arrivals.at[span, me],
            {"segment": 0, "head": other_head(step)},
        )

    share = chunks // segments

    def start_spread(span):
        def one(index, carry):
            for step in range(1, heads):
                spread(span, step, segment * share + index).start()
            return carry

        lax.fori_loop(0, share, one, 0)

    def settle_spread(span):
        await_sent(as_many(heads - 1, share), spread_sends.at[span])

    start_spread(0)
    for part in (1, 2, 0):
        loads[part].start()
    out_load.start()

    def own_copy(span):
        return pltpu.make_async_copy(
            stream_hbm.at[span], whole.at[span, :, columns_of(me)], own_sems.at[span]
        )

    @pl.when(segment == 0)
    def _():
        for span in range(spans):
            own_copy(span).start()

    for copy in fast_loads:
        copy.wait()
    for index in range(2):
        work[index] = wide_init[index]
        wide = wide_init[index].astype(jnp.float32)
        state[index] = wide
        wide_norms[index] = jnp.sqrt(jnp.sum(wide * wide, axis=0, keepdims=True))
    down = down_init[...].T
    work[2] = down
    down = down.astype(jnp.float32)
    state[2] = down
    down_norm[...] = jnp.sqrt(jnp.sum(down * down, axis=1, keepdims=True))

    def goes_straight(span, chunk):
        return chunk >= chunks - jnp.where(span > 0, 2 * unit, unit)

    def relay_copy(span, step, chunk):
        return remote(
            place(span, me, chunk),
            place(span, me, chunk),
            relay_sends.at[span],
            arrivals.at[span, me],
            {"head": other_head(step)},
        )

    def passing(side, origin, chunk):
        return remote(
            place(0, origin, chunk),
            place(0, origin, chunk),
            pass_sends.at[side, origin],
            pass_recvs.at[origin, chunk],
            {"head": me + 1 - 2 * side},
        )

    has_next = (me + 1 < heads, me >= 1)
    passed_on = chunks - 5 * unit

    def each_passing(side, distance, chunk, action):
        origin = me - distance * (1 - 2 * side)

        @pl.when(
            (chunk >= 0) & (chunk < passed_on) & (origin >= 0) & (origin < heads) & has_next[side]
        )
        def _():
            action(side, origin, chunk)

    def pass_first_block():
        def forward(side, origin, chunk):
            await_arrival(place(0, origin, chunk), pass_recvs.at[origin, chunk])
            passing(side, origin, chunk).start()

        def moment(now, carry):
            for distance in range(1, heads - 1):
                for side in range(2):
                    each_passing(side, distance, now - distance, forward)

            @pl.when(now < passed_on)
            def _():
                await_arrival(place(0, me, now), own_recvs.at[0, now])

            @pl.when((now >= passed_on) & (now < chunks))
            def _():
                relay(0, now)

            for side in range(2):
                each_passing(side, 0, now, lambda *which: passing(*which).start())
            return carry

        lax.fori_loop(0, chunks + heads - 2, moment, 0)

    def settle_first_block():
        def settle_passing(side, origin, chunk):
            await_sent(as_many(1, passed_on), pass_sends.at[side, origin])

        for distance in range(heads - 1):
            for side in range(2):
                each_passing(side, distance, 0, settle_passing)

    def relay(span, chunk):
        await_arrival(place(span, me, chunk), own_recvs.at[span, chunk])

        @pl.when(jnp.logical_not(goes_straight(span, chunk)))
        def _():
            for step in range(1, heads):
                relay_copy(span, step, chunk).start()

    def project_keys(span):
        sums[0] = jnp.zeros(sums.shape[1:], jnp.float32)
        sums[1] = jnp.zeros(sums.shape[1:], jnp.float32)

        def block(step, squares):
            origin = jnp.where(step == 0, me, other_head(heads - step))

            first = (segment > 0) & (span == 0)
            passed = jnp.where(origin < me, me + 1 < heads, me >= 1)

            @pl.when((step > 0) & jnp.logical_not(first))
            def _():
                await_arrival(whole.at[span, :, columns_of(origin)], arrivals.at[span, origin])

            @pl.when((step > 0) & first)
            def _():
                direct = pl.ds(passed_on * piece, (chunks - passed_on) * piece)
                await_arrival(
                    whole.at[span, direct, columns_of(origin)], arrivals.at[span, origin]
                )

            @pl.when((step > 0) & first & jnp.logical_not(passed))
            def _():
                def wait(chunk, carry):
                    await_arrival(place(span, origin, chunk), pass_recvs.at[origin, chunk])
                    return carry

                lax.fori_loop(0, passed_on, wait, 0)

            here = columns_of(origin)
            values = whole[span, :, here].astype(jnp.float32)
            scaled[:, here] = (values * in_gain_ref[:, here]).astype(jnp.bfloat16)
            sums[0] += dot(scaled[:, here], qkv[1, here, :])
            sums[1] += dot(scaled[:, here], qkv[2, here, :])
            return squares + jnp.sum(values * values, axis=1, keepdims=True)

        squares = lax.fori_loop(0, heads, block, jnp.zeros((rows, 1), jnp.float32))
        row_scale[...] = lax.rsqrt(squares * (1.0 / features) + norm_eps)

    def rows_at(origin, count=1):
        return pl.ds(pl.multiple_of(origin * rows, rows), count * rows)

    def far_copy(span, part, step):
        return remote(
            both.at[span, part, rows_at(place_seq), :],
            both.at[span, part, rows_at(place_seq), :],
            far_sends.at[span],
            far_recvs.at[span, part, step],
            {"seq": 2 * lax.rem(chip + step, chips) + core},
        )

    def near_copy(span, part, step):
        origin = 2 * lax.rem(chip + chips - step, chips) + core
        return remote(
            both.at[span, part, rows_at(origin), :],
            both.at[span, part, rows_at(origin), :],
            near_sends.at[span],
            near_recvs.at[span, step],
            partner,
        )

    def project_pair(span):
        project_keys(span)
        scale = row_scale[...]
        own = rows_at(place_seq)
        both[span, 0, own, :] = (rms_scale(sums[0] * scale) * qk_gain_ref[1:2, :]).astype(jnp.bfloat16)
        diagonal = lax.broadcasted_iota(jnp.int32, (rows, rows), 0) == lax.broadcasted_iota(
            jnp.int32, (rows, rows), 1
        )
        rates = jnp.sum(
            jnp.where(diagonal, rate_ref[pl.ds(span, 1), :], 0.0), axis=1, keepdims=True
        )
        both[span, 1, own, :] = (-rates * (sums[1] * scale)).astype(jnp.bfloat16)
        for part in range(2):
            for step in range(1, chips):
                far_copy(span, part, step).start()
        for part in range(2):
            near_copy(span, part, 0).start()

    def project_queries():
        queries[...] = (rms_scale(dot(scaled[...], qkv[0]) * row_scale[...]) * qk_gain_ref[0:1, :]).astype(jnp.bfloat16)

    def finish(span, chunk):
        here = rows_of(chunk)
        total = whole[span, here, columns_of(me)].astype(jnp.float32) + terms[
            span, me, here, :
        ].astype(jnp.float32)
        await_arrival(as_many(heads - 1, 1), term_recvs.at[span, chunk])
        for step in range(1, heads):
            origin = other_head(step)
            total += slots[span, origin, here, :].astype(jnp.float32)
        result_ref[span, here, :] = total.astype(jnp.bfloat16)

        @pl.when(segment < last_segment)
        def _():
            hop(span, 0, chunk).start()

            @pl.when(goes_straight(span, chunk))
            def _():
                for step in range(1, heads):
                    hop(span, step, chunk).start()

    def term_copy(span, step, chunk):
        target = other_head(step)
        return remote(
            terms.at[span, target, rows_of(chunk), :],
            slots.at[span, me, rows_of(chunk), :],
            term_sends.at[span],
            term_recvs.at[span, chunk],
            {"head": target},
        )

    def hop(span, step, chunk):
        return remote(
            result_ref.at[span, rows_of(chunk), :],
            place(span, me, chunk),
            straight_sends.at[span] if step else hop_sends.at[span],
            arrivals.at[span, me] if step else own_recvs.at[span, chunk],
            {"segment": segment + 1, "head": other_head(step) if step else me},
        )

    def finish_some(span, first, count):
        @pl.when((segment < last_segment) & (span > 0))
        def _():
            def one(index, carry):
                finish(span - 1, first + index)
                return carry

            lax.fori_loop(0, count, one, 0)

    def relay_some(span, first, count):
        @pl.when((segment > 0) & (span + 1 < spans))
        def _():
            def one(index, carry):
                relay(span + 1, first + index)
                return carry

            lax.fori_loop(0, count, one, 0)

    def gradients(span, step):
        for part in range(2):

            @pl.when(step > 0)
            def _():
                there = rows_at(2 * lax.rem(chip + chips - step, chips) + core)
                await_arrival(both.at[span, part, there, :], far_recvs.at[span, part, step])
                near_copy(span, part, step).start()

        origin = lax.rem(chip + chips - step, chips)
        await_arrival(
            both.at[span, :, rows_at(2 * origin + 1 - core), :], near_recvs.at[span, step]
        )
        here = rows_at(2 * origin, 2)
        keys = both[span, 0, here, :]
        grads = both[span, 1, here, :]
        pre_gate = dot(keys, work[0])
        pre_up = dot(keys, work[1])
        backward = dot(grads, work[2])
        sigmoid_gate = jax.nn.sigmoid(pre_gate)
        gated = pre_gate * sigmoid_gate
        rights[0, here, :] = (
            backward * pre_up * sigmoid_gate * (1.0 + pre_gate * (1.0 - sigmoid_gate))
        ).astype(jnp.bfloat16)
        rights[1, here, :] = (backward * gated).astype(jnp.bfloat16)
        rights[2, here, :] = (gated * pre_up).astype(jnp.bfloat16)

    def symmetric(upper, last_block):
        return jnp.concatenate(
            [upper, jnp.concatenate([upper[:, half:].T, last_block], axis=1)], axis=0
        )

    def mixed(gram, square):
        return (ns_second * gram.astype(jnp.float32) + ns_third * square).astype(jnp.bfloat16)

    half = work.shape[1] // 2

    def orthogonalize(span):
        raw = [contract(both[span, index // 2], rights[index], (0, 0)) for index in range(3)]
        scales = [
            1.0 / (jnp.sqrt(jnp.sum(gradient * gradient, keepdims=True)) + grad_eps)
            for gradient in raw
        ]
        for index in range(3):
            work[index] = (raw[index] * scales[index]).astype(jnp.bfloat16)

        def sweep(step, inner):
            finish_some(span, (3 + step) * unit, (1 + step) * unit)
            relay_some(span, (3 + step) * unit, (1 + step) * unit)
            current = [work[index] for index in range(3)]
            grams = [
                symmetric(
                    contract(matrix[:half], matrix, (1, 1)).astype(jnp.bfloat16),
                    contract(matrix[half:], matrix[half:], (1, 1)).astype(jnp.bfloat16),
                )
                for matrix in current
            ]
            mixings = [
                symmetric(mixed(gram[:half], dot(gram[:half], gram)), mixed(gram[half:, half:], dot(gram[half:], gram[:, half:])))
                for gram in grams
            ]
            for index in range(3):
                work[index] = (
                    ns_first * current[index].astype(jnp.float32)
                    + dot(mixings[index], current[index])
                ).astype(jnp.bfloat16)
            return inner

        lax.fori_loop(0, NS_STEPS, sweep, 0)

    def update():
        inner, wide = work.shape[1:]

        def moved(index, here, there):
            return state[index, here, there] - update_step * work[index, here, there].astype(
                jnp.float32
            )

        def store(index, here, there, fresh):
            work[index, here, there] = fresh.astype(jnp.bfloat16)
            state[index, here, there] = fresh

        for index in range(2):
            for column in range(0, wide, 256):
                there = slice(column, column + 256)
                squares = jnp.zeros((1, 256), jnp.float32)
                for row in range(0, inner, 64):
                    part = moved(index, slice(row, row + 64), there)
                    squares += jnp.sum(part * part, axis=0, keepdims=True)
                factor = wide_norms[index, :, there] / (jnp.sqrt(squares) + norm_eps)
                for row in range(0, inner, 64):
                    here = slice(row, row + 64)
                    store(index, here, there, moved(index, here, there) * factor)
        for row in range(0, inner, 32):
            here = slice(row, row + 32)
            part = moved(2, here, slice(None))
            length = jnp.sqrt(jnp.sum(part * part, axis=1, keepdims=True)) + norm_eps
            store(2, here, slice(None), part * (down_norm[here, :] / length))

    def read_out(span):
        gate_out = dot(queries[...], work[0])
        up_out = dot(queries[...], work[1])
        inner = (gate_out * jax.nn.sigmoid(gate_out) * up_out).astype(jnp.bfloat16)
        output = contract(inner, work[2], (1, 1))
        normed_out = (rms_scale(output) * out_gain_ref[...]).astype(jnp.bfloat16)

        for origin in range(heads):
            terms[span, origin] = dot(
                normed_out, out_weights[:, origin * width : (origin + 1) * width]
            ).astype(jnp.bfloat16)
    def detours(span, chunk):
        return (segment == last_segment) & (chunk >= chunks - around)

    def steps_aside(span, chunk):
        if segments == 1:
            return segment < 0
        return (segment == 0) & (span == 0) & ((chunk // unit == 2) | (chunk // unit == 4))

    def aside_chunk(place_at):
        return (2 + 2 * (place_at // unit)) * unit + lax.rem(place_at, unit)

    def aside_rows(place_at):
        return pl.ds(pl.multiple_of(place_at * piece, piece), piece)

    def aside_copy(step, place_at):
        return remote(
            terms.at[0, other_head(step), rows_of(aside_chunk(place_at)), :],
            aside.at[step, aside_rows(place_at), :],
            aside_sends.at[0],
            aside_recvs.at[place_at],
            {"segment": 1},
        )

    def aside_onward(step, place_at):
        return remote(
            aside.at[step, aside_rows(place_at), :],
            slots.at[0, me, rows_of(aside_chunk(place_at)), :],
            aside_sends.at[0],
            term_recvs.at[0, aside_chunk(place_at)],
            {"segment": 0, "head": other_head(step)},
        )

    def each_aside(action):
        def one(place_at, carry):
            for step in range(1, heads):
                action(step, place_at).start()
            return carry

        lax.fori_loop(0, 2 * unit, one, 0)

    def pass_aside():
        def one(place_at, carry):
            await_arrival(as_many(heads - 1, 1), aside_recvs.at[place_at])
            for step in range(1, heads):
                aside_onward(step, place_at).start()
            return carry

        lax.fori_loop(0, 2 * unit, one, 0)

    def settle_aside():
        await_sent(as_many(heads - 1, 2 * unit), aside_sends.at[0])

    def around_rows(chunk):
        return pl.ds(pl.multiple_of((chunk - (chunks - around)) * piece, piece), piece)

    def around_copy(span, step, chunk):
        return remote(
            terms.at[span, other_head(step), rows_of(chunk), :],
            via.at[span, step, around_rows(chunk), :],
            around_sends.at[span],
            around_recvs.at[span, chunk - (chunks - around)],
            {"segment": last_segment - 1},
        )

    def around_onward(span, step, chunk):
        return remote(
            via.at[span, step, around_rows(chunk), :],
            slots.at[span, me, rows_of(chunk), :],
            around_sends.at[span],
            term_recvs.at[span, chunk],
            {"segment": last_segment, "head": other_head(step)},
        )

    def send_terms(span):
        def send(index, carry):
            chunk = chunks - 1 - index

            @pl.when(detours(span, chunk))
            def _():
                for step in range(1, heads):
                    around_copy(span, step, chunk).start()

            return carry

        if around:
            lax.fori_loop(0, around, send, 0)

            @pl.when((segment == 0) & (span == 0))
            def _():
                each_aside(aside_copy)

        def send_straight(chunk, carry):
            @pl.when(jnp.logical_not(detours(span, chunk) | steps_aside(span, chunk)))
            def _():
                for step in range(1, heads):
                    term_copy(span, step, chunk).start()

            return carry

        lax.fori_loop(0, chunks, send_straight, 0)

    @pl.when(segment == 0)
    def _():
        for span in range(spans):
            own_copy(span).wait()

    @pl.when(segment > 0)
    def _():
        settle_spread(0)
        for span in range(1, spans):
            pl.semaphore_wait(ready, heads - 1)
            start_spread(span)
            settle_spread(span)

        @pl.when(segment == 1)
        def _():
            pass_aside()

        pass_first_block()

    for part in (1, 2, 0):
        loads[part].wait()
    out_load.wait()

    def block(span, carry):
        @pl.when((segment > 0) | (span == 0))
        def _():
            project_pair(span)

        @pl.when((segment == last_segment) & (span > 0))
        def _():
            send_terms(span - 1)

        @pl.when((segment == 0) & (span + 1 < spans))
        def _():
            start_spread(span + 1)

            for away in range(1, segments):
                for step in range(1, heads):
                    signal(ready, {"segment": away, "head": other_head(step)})

        relay_some(span, 0, unit)
        project_queries()

        def gradient_step(step, inner):
            gradients(span, step)

            @pl.when(step == 0)
            def _():
                finish_some(span, 0, unit)
                relay_some(span, unit, unit)

            return inner

        lax.fori_loop(0, chips, gradient_step, 0)
        finish_some(span, unit, 2 * unit)
        relay_some(span, 2 * unit, unit)
        orthogonalize(span)
        finish_some(span, 6 * unit, 2 * unit)

        update()
        read_out(span)
        relay_some(span, 6 * unit, 2 * unit)

        @pl.when((segment < last_segment) | (span == spans - 1))
        def _():
            send_terms(span)

        @pl.when((segment == 0) & (span + 1 < spans))
        def _():
            project_pair(span + 1)

        return carry

    lax.fori_loop(0, spans, block, 0)

    @pl.when(segment == 0)
    def _():
        for span in range(spans):
            settle_spread(span)
        if segments > 1:
            settle_aside()

    @pl.when(segment > 0)
    def _():
        settle_first_block()
        await_sent(as_many(heads - 1, chunks - unit - passed_on), relay_sends.at[0])
        for span in range(1, spans):
            await_sent(as_many(heads - 1, chunks - 2 * unit), relay_sends.at[span])

        @pl.when(segment == 1)
        def _():
            settle_aside()

    def settle_terms(span):
        beside = 2 * unit if segments > 1 and span == 0 else 0

        @pl.when((segment > 0) & (segment < last_segment))
        def _():
            await_sent(as_many(heads - 1, chunks), term_sends.at[span])

        @pl.when((segment == 0) & (segment < last_segment))
        def _():
            await_sent(as_many(heads - 1, chunks - beside), term_sends.at[span])

        @pl.when(segment == last_segment)
        def _():
            await_sent(as_many(heads - 1, chunks - around), term_sends.at[span])
            if around:
                await_sent(as_many(heads - 1, around), around_sends.at[span])

    def settle_hops(span):
        @pl.when(segment < last_segment)
        def _():
            await_sent(as_many(1, chunks), hop_sends.at[span])
            await_sent(as_many(heads - 1, 2 * unit if span else unit), straight_sends.at[span])

    for span in range(spans):
        if span + 1 < spans:
            settle_terms(span)
            settle_hops(span)
        if chips > 1:
            await_sent(both.at[span, :, pl.ds(0, (chips - 1) * rows), :], far_sends.at[span])
        await_sent(both.at[span, :, pl.ds(0, chips * rows), :], near_sends.at[span])

    def last(index, carry):
        finish(index // chunks, lax.rem(index, chunks))
        return carry

    lax.fori_loop(jnp.where(segment < last_segment, (spans - 1) * chunks, 0), spans * chunks, last, 0)

    if around:

        @pl.when(segment == last_segment - 1)
        def _():
            def pass_on(index, carry):
                span, chunk = index // around, chunks - 1 - lax.rem(index, around)
                await_arrival(
                    as_many(heads - 1, 1), around_recvs.at[span, chunk - (chunks - around)]
                )
                for step in range(1, heads):
                    around_onward(span, step, chunk).start()
                return carry

            lax.fori_loop(0, spans * around, pass_on, 0)
            for span in range(spans):
                await_sent(as_many(heads - 1, around), around_sends.at[span])

    settle_terms(spans - 1)
    settle_hops(spans - 1)


def shards(stream, in_gain, w_qkv, qk_gain, w_one, w_three, w_two, token_rate, out_gain, w_out):
    segments = lax.axis_size("segment")
    devices = lax.axis_size("seq")
    heads = lax.axis_size("head")
    spans, rows, width = stream.shape
    features = w_qkv.shape[1]
    inner, wide = w_one.shape[2:]
    tokens = devices * rows
    chunks = 8
    vmem = pl.BlockSpec(memory_space=pltpu.VMEM)
    anywhere = pl.BlockSpec(memory_space=pl.ANY)
    low = jnp.bfloat16
    dma = pltpu.SemaphoreType.DMA
    result = pl.pallas_call(
        functools.partial(step_kernel, segments, devices, heads, chunks),
        name="step",
        out_shape=jax.ShapeDtypeStruct(stream.shape, low),
        in_specs=[anywhere, vmem, anywhere, vmem, anywhere, anywhere, anywhere, vmem, vmem, anywhere],
        out_specs=vmem,
        scratch_shapes=[
            pltpu.VMEM((3, features, inner), low),
            pltpu.VMEM((inner, features), low),
            pltpu.VMEM((2, inner, wide), low),
            pltpu.VMEM((wide, inner), low),
            pltpu.VMEM((spans, rows, features), low),
            pltpu.VMEM((rows, features), low),
            pltpu.VMEM((rows, 1), jnp.float32),
            pltpu.VMEM((2, rows, inner), jnp.float32),
            pltpu.VMEM((spans, 2, tokens, inner), low),
            pltpu.VMEM((rows, inner), low),
            pltpu.VMEM((3, tokens, wide), low),
            pltpu.VMEM((3, inner, wide), low),
            pltpu.VMEM((3, inner, wide), jnp.float32),
            pltpu.VMEM((2, 1, wide), jnp.float32),
            pltpu.VMEM((inner, 1), jnp.float32),
            pltpu.VMEM((spans, heads, rows, width), low),
            pltpu.VMEM((spans, heads, rows, width), low),
            dma((3,)),
            dma((4,)),
            dma((spans,)),
            dma((spans,)),
            dma((spans, heads)),
            dma((spans, chunks)),
            dma((heads, chunks)),
            dma((spans,)),
            dma((spans, 2, devices // 2)),
            dma((spans,)),
            dma((spans, devices // 2)),
            dma((spans,)),
            dma((spans, chunks)),
            dma((spans,)),
            dma((spans,)),
            dma((spans,)),
            dma((spans,)),
            dma((spans, 3 * (chunks // 8))),
            pltpu.SemaphoreType.REGULAR,
            dma((2, heads)),
            dma((1,)),
            dma((chunks // 4,)),
            pltpu.VMEM((heads, rows // 4, width), low),
        ]
        + ([pltpu.VMEM((spans, heads, 3 * (chunks // 8) * (rows // chunks), width), low)] if segments > 1 else []),
        compiler_params=pltpu.CompilerParams(
            collective_id=0, has_side_effects=True, vmem_limit_bytes=67043328
        ),
    )(
        stream,
        in_gain,
        jnp.transpose(w_qkv[0, :, 0], (1, 0, 2)),
        qk_gain[0, 0],
        w_one[0, 0],
        w_three[0, 0],
        w_two[0, 0],
        token_rate[0],
        out_gain[0, :1],
        w_out[0, 0],
    )
    return result[None]


def solution(mesh):
    placed = (
        P(None, "seq", "head"),
        P("segment", None),
        P("segment", None, "head", None, None),
        P("segment", "head", None, None),
        P("segment", "head", None, None),
        P("segment", "head", None, None),
        P("segment", "head", None, None),
        P("segment", None, "seq"),
        P("segment", "head", None),
        P("segment", "head", None, None),
    )
    return jax.shard_map(
        shards,
        mesh=mesh,
        in_specs=placed,
        out_specs=P("segment", None, "seq", "head"),
        check_vma=False,
    )
```

```python
import functools

import jax
import jax.numpy as jnp
from jax import lax
from jax.experimental import pallas as pl
from jax.experimental.pallas import tpu as pltpu
from jax.sharding import PartitionSpec as P

NS_STEPS = 2

ns_first = 3.4445
ns_second = -4.775
ns_third = 2.0315
update_step = 1.0
norm_eps = 1e-06
grad_eps = 1e-07


def rms_scale(values):
    return values * lax.rsqrt(jnp.mean(values * values, axis=-1, keepdims=True) + norm_eps)


def dot(left, right):
    return jnp.dot(left, right, preferred_element_type=jnp.float32)


def contract(left, right, dims):
    return lax.dot_general(
        left, right, ((dims[:1], dims[1:]), ((), ())), preferred_element_type=jnp.float32
    )


def signal(semaphore, target):
    pl.semaphore_signal(
        semaphore, inc=1, device_id=target, device_id_type=pl.DeviceIdType.MESH
    )


def remote(source, target, send_sem, recv_sem, device):
    return pltpu.make_async_remote_copy(
        src_ref=source,
        dst_ref=target,
        send_sem=send_sem,
        recv_sem=recv_sem,
        device_id=device,
        device_id_type=pl.DeviceIdType.MESH,
    )


def step_kernel(
    segments,
    devices,
    heads,
    chunks,
    stream_hbm,
    in_gain_ref,
    qkv_hbm,
    qk_gain_ref,
    gate_hbm,
    up_hbm,
    down_hbm,
    rate_ref,
    out_gain_ref,
    out_hbm,
    result_ref,
    qkv,
    out_weights,
    wide_init,
    down_init,
    whole,
    scaled,
    row_scale,
    sums,
    both,
    queries,
    rights,
    work,
    state,
    wide_norms,
    down_norm,
    terms,
    slots,
    qkv_sems,
    load_sems,
    own_sems,
    spread_sends,
    arrivals,
    own_recvs,
    pass_recvs,
    far_sends,
    far_recvs,
    near_sends,
    near_recvs,
    term_sends,
    term_recvs,
    hop_sends,
    straight_sends,
    relay_sends,
    around_sends,
    around_recvs,
    ready,
    pass_sends,
    aside_sends,
    aside_recvs,
    aside,
    *vias,
):
    segment = lax.axis_index("segment")
    place_seq = lax.axis_index("seq")
    me = lax.axis_index("head")
    spans, rows, width = result_ref.shape
    features = whole.shape[2]
    chips = devices // 2
    chip, core = place_seq // 2, lax.rem(place_seq, 2)
    partner = {"seq": 2 * chip + 1 - core}
    piece = rows // chunks
    unit = chunks // 8
    around = 3 * unit if segments > 1 else 0
    via = vias[0] if around else None
    last_segment = segments - 1

    loads = [pltpu.make_async_copy(qkv_hbm.at[part], qkv.at[part], qkv_sems.at[part]) for part in range(3)]
    fast_loads = [
        pltpu.make_async_copy(gate_hbm, wide_init.at[0], load_sems.at[0]),
        pltpu.make_async_copy(up_hbm, wide_init.at[1], load_sems.at[1]),
        pltpu.make_async_copy(down_hbm, down_init, load_sems.at[2]),
    ]
    out_load = pltpu.make_async_copy(out_hbm, out_weights, load_sems.at[3])
    for copy in fast_loads:
        copy.start()

    def other_head(step):
        up, down = step - 1, heads - step
        upward = jnp.where(up >= me, up + 1, up)
        downward = jnp.where(down > me, down, down - 1)
        return jnp.where(2 * me < heads, downward, upward)

    barrier = pltpu.get_barrier_semaphore()
    for away in range(segments):
        for step in range(heads):
            if away or step:
                signal(
                    barrier,
                    {"segment": lax.rem(segment + away, segments), "head": lax.rem(me + step, heads)},
                )
    for step in range(1, chips):
        signal(barrier, {"seq": 2 * lax.rem(chip + step, chips) + core})
    signal(barrier, partner)
    pl.semaphore_wait(barrier, segments * heads - 1 + chips)

    def columns_of(origin):
        return pl.ds(pl.multiple_of(origin * width, width), width)

    def rows_of(chunk):
        if isinstance(chunk, int):
            return pl.ds(chunk * piece, piece)
        return pl.ds(pl.multiple_of(chunk * piece, piece), piece)

    def place(span, origin, chunk):
        return whole.at[span, rows_of(chunk), columns_of(origin)]

    def await_arrival(like, semaphore):
        remote(like, like, semaphore, semaphore, partner).wait_recv()

    def await_sent(like, semaphore):
        remote(like, like, semaphore, semaphore, partner).wait_send()

    def as_many(blocks, count):
        return terms.at[0, pl.ds(0, blocks), pl.ds(0, count * piece), :]

    def spread(span, step, chunk):
        return remote(
            stream_hbm.at[span, rows_of(chunk), :],
            place(span, me, chunk),
            spread_sends.at[span],
            arrivals.at[span, me],
            {"segment": 0, "head": other_head(step)},
        )

    share = chunks // segments

    def start_spread(span):
        def one(index, carry):
            for step in range(1, heads):
                spread(span, step, segment * share + index).start()
            return carry

        lax.fori_loop(0, share, one, 0)

    def settle_spread(span):
        await_sent(as_many(heads - 1, share), spread_sends.at[span])

    start_spread(0)
    for part in (1, 2, 0):
        loads[part].start()
    out_load.start()

    def own_copy(span):
        return pltpu.make_async_copy(
            stream_hbm.at[span], whole.at[span, :, columns_of(me)], own_sems.at[span]
        )

    @pl.when(segment == 0)
    def _():
        for span in range(spans):
            own_copy(span).start()

    for copy in fast_loads:
        copy.wait()
    for index in range(2):
        work[index] = wide_init[index]
        wide = wide_init[index].astype(jnp.float32)
        state[index] = wide
        wide_norms[index] = jnp.sqrt(jnp.sum(wide * wide, axis=0, keepdims=True))
    down = down_init[...].T
    work[2] = down
    down = down.astype(jnp.float32)
    state[2] = down
    down_norm[...] = jnp.sqrt(jnp.sum(down * down, axis=1, keepdims=True))

    def goes_straight(span, chunk):
        return chunk >= chunks - jnp.where(span > 0, 2 * unit, unit)

    def relay_copy(span, step, chunk):
        return remote(
            place(span, me, chunk),
            place(span, me, chunk),
            relay_sends.at[span],
            arrivals.at[span, me],
            {"head": other_head(step)},
        )

    def passing(side, origin, chunk):
        return remote(
            place(0, origin, chunk),
            place(0, origin, chunk),
            pass_sends.at[side, origin],
            pass_recvs.at[origin, chunk],
            {"head": me + 1 - 2 * side},
        )

    has_next = (me + 1 < heads, me >= 1)
    passed_on = chunks - 5 * unit

    def each_passing(side, distance, chunk, action):
        origin = me - distance * (1 - 2 * side)

        @pl.when(
            (chunk >= 0) & (chunk < passed_on) & (origin >= 0) & (origin < heads) & has_next[side]
        )
        def _():
            action(side, origin, chunk)

    def pass_first_block():
        def forward(side, origin, chunk):
            await_arrival(place(0, origin, chunk), pass_recvs.at[origin, chunk])
            passing(side, origin, chunk).start()

        def moment(now, carry):
            for distance in range(1, heads - 1):
                for side in range(2):
                    each_passing(side, distance, now - distance, forward)

            @pl.when(now < passed_on)
            def _():
                await_arrival(place(0, me, now), own_recvs.at[0, now])

            @pl.when((now >= passed_on) & (now < chunks))
            def _():
                relay(0, now)

            for side in range(2):
                each_passing(side, 0, now, lambda *which: passing(*which).start())
            return carry

        lax.fori_loop(0, chunks + heads - 2, moment, 0)

    def settle_first_block():
        def settle_passing(side, origin, chunk):
            await_sent(as_many(1, passed_on), pass_sends.at[side, origin])

        for distance in range(heads - 1):
            for side in range(2):
                each_passing(side, distance, 0, settle_passing)

    def relay(span, chunk):
        await_arrival(place(span, me, chunk), own_recvs.at[span, chunk])

        @pl.when(jnp.logical_not(goes_straight(span, chunk)))
        def _():
            for step in range(1, heads):
                relay_copy(span, step, chunk).start()

    def project_keys(span):
        sums[0] = jnp.zeros(sums.shape[1:], jnp.float32)
        sums[1] = jnp.zeros(sums.shape[1:], jnp.float32)

        def block(step, squares):
            origin = jnp.where(step == 0, me, other_head(heads - step))

            first = (segment > 0) & (span == 0)
            passed = jnp.where(origin < me, me + 1 < heads, me >= 1)

            @pl.when((step > 0) & jnp.logical_not(first))
            def _():
                await_arrival(whole.at[span, :, columns_of(origin)], arrivals.at[span, origin])

            @pl.when((step > 0) & first)
            def _():
                direct = pl.ds(passed_on * piece, (chunks - passed_on) * piece)
                await_arrival(
                    whole.at[span, direct, columns_of(origin)], arrivals.at[span, origin]
                )

            @pl.when((step > 0) & first & jnp.logical_not(passed))
            def _():
                def wait(chunk, carry):
                    await_arrival(place(span, origin, chunk), pass_recvs.at[origin, chunk])
                    return carry

                lax.fori_loop(0, passed_on, wait, 0)

            here = columns_of(origin)
            values = whole[span, :, here].astype(jnp.float32)
            scaled[:, here] = (values * in_gain_ref[:, here]).astype(jnp.bfloat16)
            sums[0] += dot(scaled[:, here], qkv[1, here, :])
            sums[1] += dot(scaled[:, here], qkv[2, here, :])
            return squares + jnp.sum(values * values, axis=1, keepdims=True)

        squares = lax.fori_loop(0, heads, block, jnp.zeros((rows, 1), jnp.float32))
        row_scale[...] = lax.rsqrt(squares * (1.0 / features) + norm_eps)

    def rows_at(origin, count=1):
        return pl.ds(pl.multiple_of(origin * rows, rows), count * rows)

    def far_copy(span, part, step):
        return remote(
            both.at[span, part, rows_at(place_seq), :],
            both.at[span, part, rows_at(place_seq), :],
            far_sends.at[span],
            far_recvs.at[span, part, step],
            {"seq": 2 * lax.rem(chip + step, chips) + core},
        )

    def near_copy(span, part, step):
        origin = 2 * lax.rem(chip + chips - step, chips) + core
        return remote(
            both.at[span, part, rows_at(origin), :],
            both.at[span, part, rows_at(origin), :],
            near_sends.at[span],
            near_recvs.at[span, step],
            partner,
        )

    def project_pair(span):
        project_keys(span)
        scale = row_scale[...]
        own = rows_at(place_seq)
        both[span, 0, own, :] = (rms_scale(sums[0] * scale) * qk_gain_ref[1:2, :]).astype(jnp.bfloat16)
        for step in range(1, chips):
            far_copy(span, 0, step).start()
        diagonal = lax.broadcasted_iota(jnp.int32, (rows, rows), 0) == lax.broadcasted_iota(
            jnp.int32, (rows, rows), 1
        )
        rates = jnp.sum(
            jnp.where(diagonal, rate_ref[pl.ds(span, 1), :], 0.0), axis=1, keepdims=True
        )
        both[span, 1, own, :] = (-rates * (sums[1] * scale)).astype(jnp.bfloat16)
        for step in range(1, chips):
            far_copy(span, 1, step).start()
        for part in range(2):
            near_copy(span, part, 0).start()

    def project_queries():
        queries[...] = (rms_scale(dot(scaled[...], qkv[0]) * row_scale[...]) * qk_gain_ref[0:1, :]).astype(jnp.bfloat16)

    def finish(span, chunk):
        here = rows_of(chunk)
        total = whole[span, here, columns_of(me)].astype(jnp.float32) + terms[
            span, me, here, :
        ].astype(jnp.float32)
        await_arrival(as_many(heads - 1, 1), term_recvs.at[span, chunk])
        for step in range(1, heads):
            origin = other_head(step)
            total += slots[span, origin, here, :].astype(jnp.float32)
        result_ref[span, here, :] = total.astype(jnp.bfloat16)

        @pl.when(segment < last_segment)
        def _():
            hop(span, 0, chunk).start()

            @pl.when(goes_straight(span, chunk))
            def _():
                for step in range(1, heads):
                    hop(span, step, chunk).start()

    def term_copy(span, step, chunk):
        target = other_head(step)
        return remote(
            terms.at[span, target, rows_of(chunk), :],
            slots.at[span, me, rows_of(chunk), :],
            term_sends.at[span],
            term_recvs.at[span, chunk],
            {"head": target},
        )

    def hop(span, step, chunk):
        return remote(
            result_ref.at[span, rows_of(chunk), :],
            place(span, me, chunk),
            straight_sends.at[span] if step else hop_sends.at[span],
            arrivals.at[span, me] if step else own_recvs.at[span, chunk],
            {"segment": segment + 1, "head": other_head(step) if step else me},
        )

    def finish_some(span, first, count):
        @pl.when((segment < last_segment) & (span > 0))
        def _():
            def one(index, carry):
                finish(span - 1, first + index)
                return carry

            lax.fori_loop(0, count, one, 0)

    def relay_some(span, first, count):
        @pl.when((segment > 0) & (span + 1 < spans))
        def _():
            def one(index, carry):
                relay(span + 1, first + index)
                return carry

            lax.fori_loop(0, count, one, 0)

    def gradients(span, step):
        for part in range(2):

            @pl.when(step > 0)
            def _():
                there = rows_at(2 * lax.rem(chip + chips - step, chips) + core)
                await_arrival(both.at[span, part, there, :], far_recvs.at[span, part, step])
                near_copy(span, part, step).start()

        origin = lax.rem(chip + chips - step, chips)
        await_arrival(
            both.at[span, :, rows_at(2 * origin + 1 - core), :], near_recvs.at[span, step]
        )
        here = rows_at(2 * origin, 2)
        keys = both[span, 0, here, :]
        grads = both[span, 1, here, :]
        pre_gate = dot(keys, work[0])
        pre_up = dot(keys, work[1])
        backward = dot(grads, work[2])
        sigmoid_gate = jax.nn.sigmoid(pre_gate)
        gated = pre_gate * sigmoid_gate
        rights[0, here, :] = (
            backward * pre_up * sigmoid_gate * (1.0 + pre_gate * (1.0 - sigmoid_gate))
        ).astype(jnp.bfloat16)
        rights[1, here, :] = (backward * gated).astype(jnp.bfloat16)
        rights[2, here, :] = (gated * pre_up).astype(jnp.bfloat16)

    def symmetric(upper, last_block):
        return jnp.concatenate(
            [upper, jnp.concatenate([upper[:, half:].T, last_block], axis=1)], axis=0
        )

    def mixed(gram, square):
        return (ns_second * gram.astype(jnp.float32) + ns_third * square).astype(jnp.bfloat16)

    half = work.shape[1] // 2

    def orthogonalize(span):
        raw = [contract(both[span, index // 2], rights[index], (0, 0)) for index in range(3)]
        scales = [
            1.0 / (jnp.sqrt(jnp.sum(gradient * gradient, keepdims=True)) + grad_eps)
            for gradient in raw
        ]
        for index in range(3):
            work[index] = (raw[index] * scales[index]).astype(jnp.bfloat16)

        def sweep(step, inner):
            finish_some(span, (3 + step) * unit, (1 + step) * unit)
            relay_some(span, (3 + step) * unit, (1 + step) * unit)
            current = [work[index] for index in range(3)]
            grams = [
                symmetric(
                    contract(matrix[:half], matrix, (1, 1)).astype(jnp.bfloat16),
                    contract(matrix[half:], matrix[half:], (1, 1)).astype(jnp.bfloat16),
                )
                for matrix in current
            ]
            mixings = [
                symmetric(mixed(gram[:half], dot(gram[:half], gram)), mixed(gram[half:, half:], dot(gram[half:], gram[:, half:])))
                for gram in grams
            ]
            for index in range(3):
                work[index] = (
                    ns_first * current[index].astype(jnp.float32)
                    + dot(mixings[index], current[index])
                ).astype(jnp.bfloat16)
            return inner

        lax.fori_loop(0, NS_STEPS, sweep, 0)

    def update():
        inner, wide = work.shape[1:]

        def moved(index, here, there):
            return state[index, here, there] - update_step * work[index, here, there].astype(
                jnp.float32
            )

        def store(index, here, there, fresh):
            work[index, here, there] = fresh.astype(jnp.bfloat16)
            state[index, here, there] = fresh

        for index in range(2):
            for column in range(0, wide, 256):
                there = slice(column, column + 256)
                squares = jnp.zeros((1, 256), jnp.float32)
                for row in range(0, inner, 64):
                    part = moved(index, slice(row, row + 64), there)
                    squares += jnp.sum(part * part, axis=0, keepdims=True)
                factor = wide_norms[index, :, there] / (jnp.sqrt(squares) + norm_eps)
                for row in range(0, inner, 64):
                    here = slice(row, row + 64)
                    store(index, here, there, moved(index, here, there) * factor)
        for row in range(0, inner, 32):
            here = slice(row, row + 32)
            part = moved(2, here, slice(None))
            length = jnp.sqrt(jnp.sum(part * part, axis=1, keepdims=True)) + norm_eps
            store(2, here, slice(None), part * (down_norm[here, :] / length))

    def read_out(span):
        gate_out = dot(queries[...], work[0])
        up_out = dot(queries[...], work[1])
        inner = (gate_out * jax.nn.sigmoid(gate_out) * up_out).astype(jnp.bfloat16)
        output = contract(inner, work[2], (1, 1))
        normed_out = (rms_scale(output) * out_gain_ref[...]).astype(jnp.bfloat16)

        for origin in range(heads):
            terms[span, origin] = dot(
                normed_out, out_weights[:, origin * width : (origin + 1) * width]
            ).astype(jnp.bfloat16)
    def detours(span, chunk):
        return (segment == last_segment) & (chunk >= chunks - around)

    def steps_aside(span, chunk):
        if segments == 1:
            return segment < 0
        return (segment == 0) & (span == 0) & ((chunk // unit == 2) | (chunk // unit == 4))

    def aside_chunk(place_at):
        return (2 + 2 * (place_at // unit)) * unit + lax.rem(place_at, unit)

    def aside_rows(place_at):
        return pl.ds(pl.multiple_of(place_at * piece, piece), piece)

    def aside_copy(step, place_at):
        return remote(
            terms.at[0, other_head(step), rows_of(aside_chunk(place_at)), :],
            aside.at[step, aside_rows(place_at), :],
            aside_sends.at[0],
            aside_recvs.at[place_at],
            {"segment": 1},
        )

    def aside_onward(step, place_at):
        return remote(
            aside.at[step, aside_rows(place_at), :],
            slots.at[0, me, rows_of(aside_chunk(place_at)), :],
            aside_sends.at[0],
            term_recvs.at[0, aside_chunk(place_at)],
            {"segment": 0, "head": other_head(step)},
        )

    def each_aside(action):
        def one(place_at, carry):
            for step in range(1, heads):
                action(step, place_at).start()
            return carry

        lax.fori_loop(0, 2 * unit, one, 0)

    def pass_aside():
        def one(place_at, carry):
            await_arrival(as_many(heads - 1, 1), aside_recvs.at[place_at])
            for step in range(1, heads):
                aside_onward(step, place_at).start()
            return carry

        lax.fori_loop(0, 2 * unit, one, 0)

    def settle_aside():
        await_sent(as_many(heads - 1, 2 * unit), aside_sends.at[0])

    def around_rows(chunk):
        return pl.ds(pl.multiple_of((chunk - (chunks - around)) * piece, piece), piece)

    def around_copy(span, step, chunk):
        return remote(
            terms.at[span, other_head(step), rows_of(chunk), :],
            via.at[span, step, around_rows(chunk), :],
            around_sends.at[span],
            around_recvs.at[span, chunk - (chunks - around)],
            {"segment": last_segment - 1},
        )

    def around_onward(span, step, chunk):
        return remote(
            via.at[span, step, around_rows(chunk), :],
            slots.at[span, me, rows_of(chunk), :],
            around_sends.at[span],
            term_recvs.at[span, chunk],
            {"segment": last_segment, "head": other_head(step)},
        )

    def send_terms(span):
        def send(index, carry):
            chunk = chunks - 1 - index

            @pl.when(detours(span, chunk))
            def _():
                for step in range(1, heads):
                    around_copy(span, step, chunk).start()

            return carry

        if around:
            lax.fori_loop(0, around, send, 0)

            @pl.when((segment == 0) & (span == 0))
            def _():
                each_aside(aside_copy)

        def send_straight(chunk, carry):
            @pl.when(jnp.logical_not(detours(span, chunk) | steps_aside(span, chunk)))
            def _():
                for step in range(1, heads):
                    term_copy(span, step, chunk).start()

            return carry

        lax.fori_loop(0, chunks, send_straight, 0)

    @pl.when(segment == 0)
    def _():
        for span in range(spans):
            own_copy(span).wait()

    @pl.when(segment > 0)
    def _():
        settle_spread(0)
        for span in range(1, spans):
            pl.semaphore_wait(ready, heads - 1)
            start_spread(span)
            settle_spread(span)

        @pl.when(segment == 1)
        def _():
            pass_aside()

        pass_first_block()

    for part in (1, 2, 0):
        loads[part].wait()
    out_load.wait()

    def block(span, carry):
        @pl.when((segment > 0) | (span == 0))
        def _():
            project_pair(span)

        @pl.when((segment == last_segment) & (span > 0))
        def _():
            send_terms(span - 1)

        @pl.when((segment == 0) & (span + 1 < spans))
        def _():
            start_spread(span + 1)

            for away in range(1, segments):
                for step in range(1, heads):
                    signal(ready, {"segment": away, "head": other_head(step)})

        relay_some(span, 0, unit)
        project_queries()

        def gradient_step(step, inner):
            gradients(span, step)

            @pl.when(step == 0)
            def _():
                finish_some(span, 0, unit)
                relay_some(span, unit, unit)

            return inner

        lax.fori_loop(0, chips, gradient_step, 0)
        finish_some(span, unit, 2 * unit)
        relay_some(span, 2 * unit, unit)
        orthogonalize(span)
        finish_some(span, 6 * unit, 2 * unit)

        update()
        read_out(span)
        relay_some(span, 6 * unit, 2 * unit)

        @pl.when((segment < last_segment) | (span == spans - 1))
        def _():
            send_terms(span)

        @pl.when((segment == 0) & (span + 1 < spans))
        def _():
            project_pair(span + 1)

        return carry

    lax.fori_loop(0, spans, block, 0)

    @pl.when(segment == 0)
    def _():
        for span in range(spans):
            settle_spread(span)
        if segments > 1:
            settle_aside()

    @pl.when(segment > 0)
    def _():
        settle_first_block()
        await_sent(as_many(heads - 1, chunks - unit - passed_on), relay_sends.at[0])
        for span in range(1, spans):
            await_sent(as_many(heads - 1, chunks - 2 * unit), relay_sends.at[span])

        @pl.when(segment == 1)
        def _():
            settle_aside()

    def settle_terms(span):
        beside = 2 * unit if segments > 1 and span == 0 else 0

        @pl.when((segment > 0) & (segment < last_segment))
        def _():
            await_sent(as_many(heads - 1, chunks), term_sends.at[span])

        @pl.when((segment == 0) & (segment < last_segment))
        def _():
            await_sent(as_many(heads - 1, chunks - beside), term_sends.at[span])

        @pl.when(segment == last_segment)
        def _():
            await_sent(as_many(heads - 1, chunks - around), term_sends.at[span])
            if around:
                await_sent(as_many(heads - 1, around), around_sends.at[span])

    def settle_hops(span):
        @pl.when(segment < last_segment)
        def _():
            await_sent(as_many(1, chunks), hop_sends.at[span])
            await_sent(as_many(heads - 1, 2 * unit if span else unit), straight_sends.at[span])

    for span in range(spans):
        if span + 1 < spans:
            settle_terms(span)
            settle_hops(span)
        if chips > 1:
            await_sent(both.at[span, :, pl.ds(0, (chips - 1) * rows), :], far_sends.at[span])
        await_sent(both.at[span, :, pl.ds(0, chips * rows), :], near_sends.at[span])

    def last(index, carry):
        finish(index // chunks, lax.rem(index, chunks))
        return carry

    lax.fori_loop(jnp.where(segment < last_segment, (spans - 1) * chunks, 0), spans * chunks, last, 0)

    if around:

        @pl.when(segment == last_segment - 1)
        def _():
            def pass_on(index, carry):
                span, chunk = index // around, chunks - 1 - lax.rem(index, around)
                await_arrival(
                    as_many(heads - 1, 1), around_recvs.at[span, chunk - (chunks - around)]
                )
                for step in range(1, heads):
                    around_onward(span, step, chunk).start()
                return carry

            lax.fori_loop(0, spans * around, pass_on, 0)
            for span in range(spans):
                await_sent(as_many(heads - 1, around), around_sends.at[span])

    settle_terms(spans - 1)
    settle_hops(spans - 1)


def shards(stream, in_gain, w_qkv, qk_gain, w_one, w_three, w_two, token_rate, out_gain, w_out):
    segments = lax.axis_size("segment")
    devices = lax.axis_size("seq")
    heads = lax.axis_size("head")
    spans, rows, width = stream.shape
    features = w_qkv.shape[1]
    inner, wide = w_one.shape[2:]
    tokens = devices * rows
    chunks = 8
    vmem = pl.BlockSpec(memory_space=pltpu.VMEM)
    anywhere = pl.BlockSpec(memory_space=pl.ANY)
    low = jnp.bfloat16
    dma = pltpu.SemaphoreType.DMA
    result = pl.pallas_call(
        functools.partial(step_kernel, segments, devices, heads, chunks),
        name="step",
        out_shape=jax.ShapeDtypeStruct(stream.shape, low),
        in_specs=[anywhere, vmem, anywhere, vmem, anywhere, anywhere, anywhere, vmem, vmem, anywhere],
        out_specs=vmem,
        scratch_shapes=[
            pltpu.VMEM((3, features, inner), low),
            pltpu.VMEM((inner, features), low),
            pltpu.VMEM((2, inner, wide), low),
            pltpu.VMEM((wide, inner), low),
            pltpu.VMEM((spans, rows, features), low),
            pltpu.VMEM((rows, features), low),
            pltpu.VMEM((rows, 1), jnp.float32),
            pltpu.VMEM((2, rows, inner), jnp.float32),
            pltpu.VMEM((spans, 2, tokens, inner), low),
            pltpu.VMEM((rows, inner), low),
            pltpu.VMEM((3, tokens, wide), low),
            pltpu.VMEM((3, inner, wide), low),
            pltpu.VMEM((3, inner, wide), jnp.float32),
            pltpu.VMEM((2, 1, wide), jnp.float32),
            pltpu.VMEM((inner, 1), jnp.float32),
            pltpu.VMEM((spans, heads, rows, width), low),
            pltpu.VMEM((spans, heads, rows, width), low),
            dma((3,)),
            dma((4,)),
            dma((spans,)),
            dma((spans,)),
            dma((spans, heads)),
            dma((spans, chunks)),
            dma((heads, chunks)),
            dma((spans,)),
            dma((spans, 2, devices // 2)),
            dma((spans,)),
            dma((spans, devices // 2)),
            dma((spans,)),
            dma((spans, chunks)),
            dma((spans,)),
            dma((spans,)),
            dma((spans,)),
            dma((spans,)),
            dma((spans, 3 * (chunks // 8))),
            pltpu.SemaphoreType.REGULAR,
            dma((2, heads)),
            dma((1,)),
            dma((chunks // 4,)),
            pltpu.VMEM((heads, rows // 4, width), low),
        ]
        + ([pltpu.VMEM((spans, heads, 3 * (chunks // 8) * (rows // chunks), width), low)] if segments > 1 else []),
        compiler_params=pltpu.CompilerParams(
            collective_id=0, has_side_effects=True, vmem_limit_bytes=67043328
        ),
    )(
        stream,
        in_gain,
        jnp.transpose(w_qkv[0, :, 0], (1, 0, 2)),
        qk_gain[0, 0],
        w_one[0, 0],
        w_three[0, 0],
        w_two[0, 0],
        token_rate[0],
        out_gain[0, :1],
        w_out[0, 0],
    )
    return result[None]


def solution(mesh):
    placed = (
        P(None, "seq", "head"),
        P("segment", None),
        P("segment", None, "head", None, None),
        P("segment", "head", None, None),
        P("segment", "head", None, None),
        P("segment", "head", None, None),
        P("segment", "head", None, None),
        P("segment", None, "seq"),
        P("segment", "head", None),
        P("segment", "head", None, None),
    )
    return jax.shard_map(
        shards,
        mesh=mesh,
        in_specs=placed,
        out_specs=P("segment", None, "seq", "head"),
        check_vma=False,
    )
```
